128 devices in a mesh: seq: 16 (over x, y_lo, core), head: 8 (over z, y_hi).
Axes of the slice: x: 4, y: 4 (y_hi: 2, y_lo: 2; y = y_hi * 2 + y_lo), z: 4, core: 2. Of those that a mesh axis runs over, the one named last changes fastest.
Arguments:
- queries: bfloat16 [12288, 2048], P(('seq', 'head')), may hold values from -8 to 8
- keys: bfloat16 [12288, 2048], P(('seq', 'head')), may hold values from -8 to 8
- values: bfloat16 [12288, 2048], P(('seq', 'head')), may hold values from -6 to 6
- cotangent: bfloat16 [12288, 2048], P(('seq', 'head')), may hold values from -6 to 6
- neighbours: int32 [192, 27], replicated, may hold values from -1 to 191, as said below
Outputs:
- output: bfloat16 [12288, 2048], P(('seq', 'head'))
- grad_query: bfloat16 [12288, 2048], P(('seq', 'head'))
- grad_key: bfloat16 [12288, 2048], P(('seq', 'head'))
- grad_value: bfloat16 [12288, 2048], P(('seq', 'head'))
The draws below stay inside these ranges and needn't reach their ends.
Inputs may be any that keep to these rules, and one draw needn't show every extreme that they name: `neighbours`: row g lists distinct tiles, always g itself; a listed tile's frame, tile row and tile column each differ from g's by at most one; -1 marks an empty slot; slots stand in any order.
All inputs are finite; a program needn't handle non-finite values.
Results may differ from the reference program's by a relative error of at most 0.015.
Values may be sent and summed in bfloat16 or wider, within the bound.
No kernel may reach another device: no remote copies, remote signals or barrier semaphores. Data moves between devices by JAX's collectives and lax.ppermute only.
A program may use at most 128 MiB of HBM per device.

```python
import math
import jax
import jax.numpy as jnp
from jax import lax

TILE = 64
TILE_ROWS = 3
TILE_COLS = 4
TILES_F = 12
SLOTS = 27
HEADS = 16
HD = 128
FRAMES = 16
TILES = 192
TOKENS = 12288


def shared_pair(key):
    key_query, key_keys = jax.random.split(key, 2)
    width_all = HEADS * HD
    query_draw = 1.5 * jnp.clip(jax.random.normal(key_query, (TOKENS, width_all), jnp.float32), -3.3, 3.3)
    keys_draw = 1.5 * jnp.clip(jax.random.normal(key_keys, (TOKENS, width_all), jnp.float32), -3.3, 3.3)
    return (query_draw, keys_draw)


def draw_queries(key, part):
    query_draw, keys_draw = shared_pair(jax.random.fold_in(key, 7))
    return query_draw.astype(jnp.bfloat16)


def draw_keys(key, part):
    query_draw, keys_draw = shared_pair(jax.random.fold_in(key, 7))
    return keys_draw.astype(jnp.bfloat16)


def draw_neighbours(key, part):
    key_drop, key_order = jax.random.split(jax.random.fold_in(key, 13))
    tile_ids = jnp.arange(TILES, dtype=jnp.int32)
    frame = tile_ids // TILES_F
    tile_row = tile_ids % TILES_F // TILE_COLS
    tile_col = tile_ids % TILE_COLS
    slot = jnp.arange(SLOTS, dtype=jnp.int32)
    step_frame = slot // 9 - 1
    step_row = slot // 3 % 3 - 1
    step_col = slot % 3 - 1
    near_frame = frame[:, None] + step_frame[None, :]
    near_row = tile_row[:, None] + step_row[None, :]
    near_col = tile_col[:, None] + step_col[None, :]
    inside = (near_frame >= 0) & (near_frame < FRAMES) & (near_row >= 0) & (near_row < TILE_ROWS) & (near_col >= 0) & (near_col < TILE_COLS)
    kept = (jax.random.randint(key_drop, (TILES, SLOTS), 0, 4) > 0) | (slot[None, :] == 13)
    listed = jnp.where(inside & kept, near_frame * TILES_F + near_row * TILE_COLS + near_col, -1)
    order_keys = jax.random.randint(key_order, (TILES, SLOTS), 0, 1 << 20) * 32 + slot[None, :]
    order = jnp.argsort(order_keys, axis=1)
    return jnp.take_along_axis(listed, order, axis=1).astype(jnp.int32)


def shard_levels(key, extent, cuts, low, top_value):
    factor_of, own = 1.0, jax.random.fold_in(key, 6)
    for dim, parts in cuts:
        steps = jnp.exp(jax.random.uniform(jax.random.fold_in(own, dim), (parts,), jnp.float32, low / len(cuts), top_value / len(cuts)))
        factor_of = factor_of * jnp.repeat(steps, extent[dim] // parts).reshape([-1 if axis == dim else 1 for axis in range(len(extent))])
    return factor_of


def normal_values(stream_key, dims, width, bound, cuts=(), kind=jnp.bfloat16):
    entries = jax.random.normal(stream_key, dims, jnp.float32) * width
    if len(cuts) > 0:
        entries = shard_levels(stream_key, dims, cuts, -0.22, 0.18) * entries
    return jnp.clip(entries, min=-bound, max=bound).astype(kind)


def setup_inputs(seed: int = 0) -> dict:
    key_list = jax.random.split(jax.random.key(seed), 6)
    return {
        "queries": draw_queries(jax.random.fold_in(key_list[5], 71), 0),
        "keys": draw_keys(jax.random.fold_in(key_list[5], 71), 0),
        "values": normal_values(key_list[2], (TOKENS, HEADS * HD), 1.0, 6.0, ((0, 128),)),
        "cotangent": normal_values(key_list[3], (TOKENS, HEADS * HD), 1.0, 6.0, ((0, 128),)),
        "neighbours": draw_neighbours(jax.random.fold_in(key_list[5], 71), 0),
    }


masked_score = -1e+30

def attend_tiles(query_blk, kv_near, key_mask, cot_blk, head_count):
    block_tiles, tile_len, feature_width = query_blk.shape
    key_len = kv_near.shape[1]
    head_size = feature_width // head_count
    score_scale = 1.0 / math.sqrt(head_size)
    highest = lax.Precision.HIGHEST
    query_heads = query_blk.astype(jnp.float32).reshape(block_tiles, tile_len, head_count, head_size)
    key_heads = kv_near[:, :, :feature_width].astype(jnp.float32).reshape(block_tiles, key_len, head_count, head_size)
    value_heads = kv_near[:, :, feature_width:].astype(jnp.float32).reshape(block_tiles, key_len, head_count, head_size)
    cot_heads = cot_blk.astype(jnp.float32).reshape(block_tiles, tile_len, head_count, head_size)
    scores = jnp.einsum('btnd,bknd->bntk', query_heads, key_heads, precision=highest) * score_scale
    scores = jnp.where(key_mask[:, None, None, :], scores, masked_score)
    row_max = lax.optimization_barrier(jnp.max(scores, axis=-1, keepdims=True))
    log_total = row_max + jnp.log(lax.optimization_barrier(jnp.sum(jnp.exp(scores - row_max), axis=-1, keepdims=True)))
    probs = jnp.exp(scores - log_total)
    probs_low = probs.astype(jnp.bfloat16)
    output = jnp.einsum('bntk,bknd->btnd', probs_low.astype(jnp.float32), value_heads, precision=highest).astype(jnp.bfloat16)
    grad_dot = lax.optimization_barrier(jnp.sum(cot_heads * output.astype(jnp.float32), axis=-1))
    grad_prob = jnp.einsum('btnd,bknd->bntk', cot_heads, value_heads, precision=highest)
    grad_score = (probs * (grad_prob - jnp.transpose(grad_dot, (0, 2, 1))[..., None]) * score_scale).astype(jnp.bfloat16)
    grad_query = jnp.einsum('bntk,bknd->btnd', grad_score.astype(jnp.float32), key_heads, precision=highest).astype(jnp.bfloat16)
    grad_key = jnp.einsum('bntk,btnd->bknd', grad_score.astype(jnp.float32), query_heads, precision=highest)
    grad_value = jnp.einsum('bntk,btnd->bknd', probs_low.astype(jnp.float32), cot_heads, precision=highest)
    grad_pair = jnp.concatenate([grad_key.reshape(block_tiles, key_len, feature_width), grad_value.reshape(block_tiles, key_len, feature_width)], axis=-1)
    return (output.reshape(block_tiles, tile_len, feature_width), grad_query.reshape(block_tiles, tile_len, feature_width), grad_pair)

def reference(queries, keys, values, cotangent, neighbours):
    feature_width = queries.shape[1]
    query_tiles = queries.reshape(TILES, TILE, feature_width)
    cot_tiles = cotangent.reshape(TILES, TILE, feature_width)
    pair_tiles = jnp.concatenate([keys, values], axis=1).reshape(TILES, TILE, 2 * feature_width)
    pair_tiles = jnp.concatenate([pair_tiles, jnp.zeros((1, TILE, 2 * feature_width), pair_tiles.dtype)], axis=0)
    listed = neighbours >= 0
    slot_index = jnp.where(listed, neighbours, TILES).astype(jnp.int32)
    block_tiles = TILES_F // 4

    def one_block(grad_buffer, block_id):
        first_tile = (block_id * block_tiles).astype(jnp.int32)
        query_blk = lax.dynamic_slice_in_dim(query_tiles, first_tile, block_tiles, 0)
        cot_blk = lax.dynamic_slice_in_dim(cot_tiles, first_tile, block_tiles, 0)
        index_blk = lax.dynamic_slice_in_dim(slot_index, first_tile, block_tiles, 0)
        listed_blk = lax.dynamic_slice_in_dim(listed, first_tile, block_tiles, 0)
        kv_near = jnp.take(pair_tiles, index_blk, axis=0).reshape(block_tiles, SLOTS * TILE, 2 * feature_width)
        key_mask = jnp.repeat(listed_blk, TILE, axis=1)
        output, grad_query, grad_pair = attend_tiles(query_blk, kv_near, key_mask, cot_blk, HEADS)
        grad_buffer = grad_buffer.at[index_blk].add(grad_pair.reshape(block_tiles, SLOTS, TILE, 2 * feature_width))
        return (grad_buffer, (output, grad_query))
    start_buffer = jnp.zeros((TILES + 1, TILE, 2 * feature_width), jnp.float32)
    grad_buffer, (outputs, grad_queries) = lax.scan(one_block, start_buffer, jnp.arange(TILES // block_tiles, dtype=jnp.int32))
    output = outputs.reshape(TOKENS, feature_width)
    grad_query = grad_queries.reshape(TOKENS, feature_width)
    grad_rows = grad_buffer[:TILES].reshape(TOKENS, 2 * feature_width)
    return (output, grad_query, grad_rows[:, :feature_width].astype(jnp.bfloat16), grad_rows[:, feature_width:].astype(jnp.bfloat16))
```

```python
import functools
import math

import jax
import jax.numpy as jnp
from jax import lax
from jax.experimental import pallas as pl
from jax.experimental.pallas import tpu as pltpu
from jax.sharding import Mesh, PartitionSpec as P

TILE = 64
TILES_F = 12
HD = 128
FRAME = TILE * TILES_F
BLOCK = 4 * TILE
SLOTS_F = 5
CHUNKS = 8
CHUNK = FRAME // CHUNKS
PLANE = 16
MASKED = -1e30
SCALE = 1.0 / math.sqrt(HD)
LOG2E = 1.4426950408889634
ANY = pl.BlockSpec(memory_space=pl.ANY)
F32 = jnp.float32
BF16 = jnp.bfloat16


def pack_kernel(q_ref, k_ref, v_ref, c_ref, out_ref):
    for a, ref in enumerate((q_ref, k_ref, v_ref, c_ref)):
        for g in range(PLANE):
            out_ref[g, a] = ref[:, g * HD : (g + 1) * HD]


def pack(q, k, v, c):
    return pl.pallas_call(
        pack_kernel,
        out_shape=jax.ShapeDtypeStruct((PLANE, 4, CHUNK, HD), BF16),
        name="pack",
    )(q, k, v, c)


def unpack_kernel(in_ref, *out_refs):
    for a, ref in enumerate(out_refs):
        for g in range(PLANE):
            ref[:, g * HD : (g + 1) * HD] = in_ref[g, a]


def unpack(packed):
    shape = jax.ShapeDtypeStruct((CHUNK, PLANE * HD), BF16)
    return pl.pallas_call(unpack_kernel, out_shape=(shape,) * 4, name="unpack")(packed)


def nt(a, b):
    return lax.dot_general(a, b, (((1,), (1,)), ((), ())), preferred_element_type=F32)


def nn(a, b):
    return lax.dot_general(a, b, (((1,), (0,)), ((), ())), preferred_element_type=F32)


def tn(a, b):
    return lax.dot_general(a, b, (((0,), (0,)), ((), ())), preferred_element_type=F32)


def group_rows(x):
    return x.reshape(x.shape[0] // 8, 8, x.shape[1])


def attend_kernel(
    core_ref, mine_ref, swap_ref, edge_ref, bias_ref,
    packed_ref, gswap_ref, gedge_ref, gown_ref,
    q_s, c_s, k_s, v_s, s_s, p_s, d_s, o_s, dq_s, dk_s, dv_s, gb_s, sems, out_sems,
):
    core = core_ref[0]

    def copy(src, dst, n):
        return pltpu.make_async_copy(src, dst, sems.at[n])

    def mine(frame, a):
        return mine_ref.at[pl.ds(frame * CHUNKS, CHUNKS), a]

    fixed = []
    for f in range(2):
        fixed.append(copy(mine(f, 0), q_s.at[f], f))
        fixed.append(copy(mine(f, 3), c_s.at[f], 2 + f))
        fixed.append(copy(mine(f, 1), k_s.at[1 + 2 * f], 4 + f))
        fixed.append(copy(mine(f, 2), v_s.at[1 + 2 * f], 6 + f))
    for cp in fixed:
        cp.start()

    def halo_copies(which):
        slots = ((2, 4), 0) if which == 0 else ((0, 2), 4)
        cps = []
        for a, dst in enumerate((k_s, v_s)):
            for f in range(2):
                src = swap_ref.at[pl.ds(f * CHUNKS, CHUNKS), a]
                cps.append(copy(src, dst.at[slots[0][f]], 8 + 2 * a + f))
            cps.append(copy(edge_ref.at[:, a], dst.at[slots[1]], 12 + a))
        return cps

    for which in range(2):
        @pl.when(core == which)
        def _():
            for cp in halo_copies(which):
                cp.start()

    dk_s[...] = jnp.zeros_like(dk_s)
    dv_s[...] = jnp.zeros_like(dv_s)
    for cp in fixed:
        cp.wait()
    for cp in halo_copies(0):
        cp.wait()

    qf = q_s.reshape(2 * FRAME, HD)
    cf = c_s.reshape(2 * FRAME, HD)
    kf = k_s.reshape(SLOTS_F * FRAME, HD)
    vf = v_s.reshape(SLOTS_F * FRAME, HD)
    of = o_s.reshape(2 * FRAME, HD)
    dqf = dq_s.reshape(2 * FRAME, HD)

    def frame_step(f, carry):
        for r in range(3):
            lo, n = ((0, 2 * BLOCK), (0, 3 * BLOCK), (BLOCK, 2 * BLOCK))[r]
            rows = pl.ds(pl.multiple_of(f * FRAME + r * BLOCK, BLOCK), BLOCK)
            q = qf[rows, :]
            c = cf[rows, :]

            def keys(s):
                return pl.ds(pl.multiple_of((2 * f + s) * FRAME + lo, BLOCK), n)

            top = None
            for s in range(3):
                st = nt(kf[keys(s), :], q)
                for t in range(n // TILE):
                    tile = (2 * f + s) * TILES_F + lo // TILE + t
                    x = st[t * TILE : (t + 1) * TILE] + bias_ref[pl.ds(tile, 1), pl.ds(pl.multiple_of(f * FRAME + r * BLOCK, BLOCK), BLOCK)]
                    s_s[s * n + t * TILE : s * n + (t + 1) * TILE, :] = x
                    part = jnp.max(group_rows(x), axis=0)
                    top = part if top is None else jnp.maximum(top, part)
            top = jnp.max(top, axis=0, keepdims=True) * (SCALE * LOG2E)
            total = jnp.zeros((8, BLOCK), F32)
            for t in range(3 * n // TILE):
                sl = slice(t * TILE, (t + 1) * TILE)
                e = jnp.exp2(s_s[sl, :] * (SCALE * LOG2E) - top)
                s_s[sl, :] = e
                total = total + jnp.sum(group_rows(e), axis=0)
            inv = 1.0 / jnp.sum(total, axis=0, keepdims=True)
            for t in range(3 * n // TILE):
                sl = slice(t * TILE, (t + 1) * TILE)
                p_s[sl, :] = (s_s[sl, :] * inv).astype(BF16)
            o = None
            for s in range(3):
                part = tn(p_s[s * n : (s + 1) * n, :], vf[keys(s), :])
                o = part if o is None else o + part
            o = o.astype(BF16)
            of[rows, :] = o
            dots = jnp.sum((c.astype(F32) * o.astype(F32)).T, axis=0, keepdims=True)
            inv_scale = inv * SCALE
            dq = None
            for s in range(3):
                dp = nt(vf[keys(s), :], c)
                for t in range(n // TILE):
                    sl = slice(s * n + t * TILE, s * n + (t + 1) * TILE)
                    d_s[sl, :] = (s_s[sl, :] * inv_scale * (dp[t * TILE : (t + 1) * TILE] - dots)).astype(BF16)
                dv_s[keys(s), :] += nn(p_s[s * n : (s + 1) * n, :], c)
                dk_s[keys(s), :] += nn(d_s[s * n : (s + 1) * n, :], q)
                part = tn(d_s[s * n : (s + 1) * n, :], kf[keys(s), :])
                dq = part if dq is None else dq + part
            dqf[rows, :] = dq.astype(BF16)
        return carry

    lax.fori_loop(0, 2, frame_step, 0)

    outs = []

    def out_copy(src, dst):
        cp = pltpu.make_async_copy(src, dst, out_sems.at[len(outs)])
        cp.start()
        outs.append(cp)

    for f in range(2):
        out_copy(o_s.at[f], packed_ref.at[pl.ds(f * CHUNKS, CHUNKS), 0])
        out_copy(dq_s.at[f], packed_ref.at[pl.ds(f * CHUNKS, CHUNKS), 1])
    for a, acc in enumerate((dk_s, dv_s)):
        for f in range(2):
            out_copy(acc.at[pl.ds((1 + 2 * f) * FRAME, FRAME)], gown_ref.at[f, a])
        for i, first in enumerate((2, 4)):
            slot = first - 2 * core
            gb_s[a, i] = acc[pl.ds(pl.multiple_of(slot * FRAME, FRAME), FRAME), :].astype(BF16)
            out_copy(gb_s.at[a, i], gswap_ref.at[i, a])
        gb_s[a, 2] = acc[pl.ds(pl.multiple_of(4 * core * FRAME, FRAME), FRAME), :].astype(BF16)
        out_copy(gb_s.at[a, 2], gedge_ref.at[a])
    for cp in outs:
        cp.wait()


def attend(core, mine, swap, edge, bias):
    tokens = 2 * FRAME
    return pl.pallas_call(
        attend_kernel,
        in_specs=[pl.BlockSpec(memory_space=pltpu.SMEM), ANY, ANY, ANY, pl.BlockSpec(memory_space=pltpu.VMEM)],
        out_specs=(ANY,) * 4,
        out_shape=(
            jax.ShapeDtypeStruct((PLANE, 4, CHUNK, HD), BF16),
            jax.ShapeDtypeStruct((2, 2, FRAME, HD), BF16),
            jax.ShapeDtypeStruct((2, FRAME, HD), BF16),
            jax.ShapeDtypeStruct((2, 2, FRAME, HD), F32),
        ),
        scratch_shapes=[
            pltpu.VMEM((2, CHUNKS, CHUNK, HD), BF16),
            pltpu.VMEM((2, CHUNKS, CHUNK, HD), BF16),
            pltpu.VMEM((SLOTS_F, CHUNKS, CHUNK, HD), BF16),
            pltpu.VMEM((SLOTS_F, CHUNKS, CHUNK, HD), BF16),
            pltpu.VMEM((9 * BLOCK, BLOCK), F32),
            pltpu.VMEM((9 * BLOCK, BLOCK), BF16),
            pltpu.VMEM((9 * BLOCK, BLOCK), BF16),
            pltpu.VMEM((2, CHUNKS, CHUNK, HD), BF16),
            pltpu.VMEM((2, CHUNKS, CHUNK, HD), BF16),
            pltpu.VMEM((SLOTS_F * FRAME, HD), F32),
            pltpu.VMEM((SLOTS_F * FRAME, HD), F32),
            pltpu.VMEM((2, 3, FRAME, HD), BF16),
            pltpu.SemaphoreType.DMA((14,)),
            pltpu.SemaphoreType.DMA((14,)),
        ],
        name="attend",
    )(core, mine, swap, edge, bias)


def join_kernel(core_ref, packed_ref, own_ref, swap_ref, edge_ref, out_ref, sum_s, sems):
    core = core_ref[0]
    outs = []
    for f in range(2):
        here = jnp.where(core == f, 1.0, 0.0)
        for a in range(2):
            for h in range(CHUNKS):
                sl = slice(h * CHUNK, (h + 1) * CHUNK)
                x = own_ref[f, a, sl, :] + swap_ref[f, a, sl, :].astype(F32)
                x = x + edge_ref[a, sl, :].astype(F32) * here
                sum_s[f, a, h] = x.astype(BF16)
            cp = pltpu.make_async_copy(
                sum_s.at[f, a], out_ref.at[pl.ds(f * CHUNKS, CHUNKS), 2 + a], sems.at[2 * f + a]
            )
            cp.start()
            outs.append(cp)
    for cp in outs:
        cp.wait()


def join(core, packed, own, swap, edge):
    vmem = pl.BlockSpec(memory_space=pltpu.VMEM)
    return pl.pallas_call(
        join_kernel,
        in_specs=[pl.BlockSpec(memory_space=pltpu.SMEM), ANY, vmem, vmem, vmem],
        out_specs=ANY,
        out_shape=jax.ShapeDtypeStruct((PLANE, 4, CHUNK, HD), BF16),
        scratch_shapes=[pltpu.VMEM((2, 2, CHUNKS, CHUNK, HD), BF16), pltpu.SemaphoreType.DMA((4,))],
        input_output_aliases={1: 0},
        name="join",
    )(core, packed, own, swap, edge)


def tile_bias(neighbours, first, base):
    rows = jnp.concatenate(
        [lax.dynamic_slice_in_dim(neighbours, first + 2 * f * TILES_F, TILES_F, 0) for f in range(2)], axis=0
    )
    rel = jnp.where(rows >= 0, rows - base, -1)
    tiles = jnp.arange(SLOTS_F * TILES_F, dtype=jnp.int32)
    hit = jnp.any(rel[None, :, :] == tiles[:, None, None], axis=2)
    return jnp.repeat(jnp.where(hit, 0.0, MASKED).astype(F32), TILE, axis=1)


def shards(queries, keys, values, cotangent, neighbours):
    plane = ("yl", "head")
    ring = lax.axis_size("sx")
    across = []
    for i in range(ring - 1):
        across.append((2 * i + 1, 2 * i + 2))
        across.append((2 * i + 2, 2 * i + 1))
    swap_pairs = [(0, 1), (1, 0)]
    core = lax.axis_index("co")
    x = lax.axis_index("sx")
    first = (4 * x + core) * TILES_F
    bias = tile_bias(neighbours, first, first - TILES_F)
    core_arr = jnp.full((1,), core, jnp.int32)

    mine = lax.all_to_all(pack(queries, keys, values, cotangent), plane, split_axis=0, concat_axis=0, tiled=True)
    kv = mine[:, 1:3]
    kv_edge = lax.dynamic_slice_in_dim(kv, core * CHUNKS, CHUNKS, 0)
    edge = lax.ppermute(kv_edge, ("sx", "co"), across)
    swap = lax.ppermute(kv, "co", swap_pairs)
    packed, gswap, gedge, gown = attend(core_arr, mine, swap, edge, bias)
    gedge_in = lax.ppermute(gedge, ("sx", "co"), across)
    gswap_in = lax.ppermute(gswap, "co", swap_pairs)
    packed = join(core_arr, packed, gown, gswap_in, gedge_in)
    return unpack(lax.all_to_all(packed, plane, split_axis=0, concat_axis=0, tiled=True))


def solution(mesh):
    view = Mesh(mesh.devices.reshape(mesh.devices.shape[0] // 4, 2, 2, -1), ("sx", "yl", "co", "head"))
    rows = P(("sx", "yl", "co", "head"), None)
    return jax.shard_map(
        shards,
        mesh=view,
        in_specs=(rows,) * 4 + (P(),),
        out_specs=(rows,) * 4,
        check_vma=False,
    )
```

```python
import functools
import math

import jax
import jax.numpy as jnp
from jax import lax
from jax.experimental import pallas as pl
from jax.experimental.pallas import tpu as pltpu
from jax.sharding import Mesh, PartitionSpec as P

TILE = 64
TILES_F = 12
HD = 128
FRAME = TILE * TILES_F
BLOCK = 4 * TILE
KEYS = 3 * FRAME
CHUNKS = 8
CHUNK = FRAME // CHUNKS
PLANE = 16
MASKED = -1e30
SCALE = 1.0 / math.sqrt(HD)
LOG2E = 1.4426950408889634
ANY = pl.BlockSpec(memory_space=pl.ANY)
F32 = jnp.float32
BF16 = jnp.bfloat16


def pack_kernel(q_ref, k_ref, v_ref, c_ref, out_ref):
    for a, ref in enumerate((q_ref, k_ref, v_ref, c_ref)):
        for g in range(PLANE):
            out_ref[g, a] = ref[:, g * HD : (g + 1) * HD]


def pack(q, k, v, c):
    return pl.pallas_call(
        pack_kernel,
        out_shape=jax.ShapeDtypeStruct((PLANE, 4, CHUNK, HD), BF16),
        name="pack",
    )(q, k, v, c)


def unpack_kernel(in_ref, *out_refs):
    for a, ref in enumerate(out_refs):
        for g in range(PLANE):
            ref[:, g * HD : (g + 1) * HD] = in_ref[g, a]


def unpack(packed):
    shape = jax.ShapeDtypeStruct((CHUNK, PLANE * HD), BF16)
    return pl.pallas_call(unpack_kernel, out_shape=(shape,) * 2, name="unpack")(packed)


def nt(a, b):
    return lax.dot_general(a, b, (((1,), (1,)), ((), ())), preferred_element_type=F32)


def nn(a, b):
    return lax.dot_general(a, b, (((1,), (0,)), ((), ())), preferred_element_type=F32)


def group_rows(x):
    return x.reshape(x.shape[0] // 8, 8, x.shape[1])


def marks(shape, dim, row):
    return (lax.broadcasted_iota(jnp.int32, shape, dim) == row).astype(F32)


SPANS = ((0, 2 * BLOCK), (0, 3 * BLOCK), (BLOCK, 2 * BLOCK))


def attend_kernel(edge, core_ref, *refs):
    refs = list(refs)
    mine_ref, swap_ref = refs[:2]
    del refs[:2]
    edge_ref = refs.pop(0) if edge else None
    bias_ref = refs.pop(0)
    if edge:
        old_swap_ref = refs[2]
        del refs[:3]
    out_ref, gown_ref, gswap_ref = refs[:3]
    del refs[:3]
    gedge_ref = refs.pop(0) if edge else None
    (q_s, c_s, k_s, v_s, hot_s, kt_s, vt_s, qt_s, ct_s, s_s, p_s, d_s, o_s, dq_s, gb_s, old_s, sems, out_sems) = refs

    core = core_ref[0]
    frame = core if edge else 1 - core

    def part(ref, index, a):
        return ref.at[pl.ds(index * CHUNKS, CHUNKS), a]

    ins = {}

    def load(name, src, dst):
        cp = pltpu.make_async_copy(src, dst, sems.at[len(ins)])
        cp.start()
        ins[name] = cp

    load("q", part(mine_ref, frame, 0), q_s)
    for a, dst in ((1, k_s), (2, v_s)):
        load((a, 1), part(mine_ref, frame, a), dst.at[1])
        if edge:
            load((a, 0), edge_ref.at[:, a - 1], dst.at[0])
            load((a, 2), part(swap_ref, core, a - 1), dst.at[2])
        else:
            load((a, 0), part(swap_ref, 0, a - 1), dst.at[0])
            load((a, 2), part(swap_ref, 1, a - 1), dst.at[2])
    load("c", part(mine_ref, frame, 3), c_s)
    if edge:
        for a in range(2):
            load(("old", a), part(old_swap_ref, core, a), old_s.at[a])

    lane = lax.broadcasted_iota(jnp.int32, (TILE, HD), 1)
    for t in range(3 * TILES_F):
        hot_s[t * TILE : (t + 1) * TILE, :] = (lane == t).astype(F32).astype(BF16)
    qt_s[HD:, :] = bias_ref[...]
    vt_s[HD:, :] = marks((16, KEYS), 0, 0).astype(BF16)
    for cp in ins.values():
        cp.wait()

    qf = q_s.reshape(FRAME, HD)
    cf = c_s.reshape(FRAME, HD)
    kf = k_s.reshape(KEYS, HD)
    vf = v_s.reshape(KEYS, HD)
    of = o_s.reshape(FRAME, HD)
    dqf = dq_s.reshape(FRAME, HD)
    gf = gb_s.reshape(2 * KEYS, HD)
    oldf = old_s.reshape(2 * FRAME, HD)

    qt_s[:HD, :] = qf[...].T

    def keys(s, lo, n):
        return slice(s * FRAME + lo, s * FRAME + lo + n)

    tops = {}

    def score(r):
        lo, n = SPANS[r]
        cols = slice(r * BLOCK, (r + 1) * BLOCK)
        qt = qt_s[:, cols]
        top = None
        for s in range(3):
            for b in range(n // BLOCK):
                ks = keys(s, lo + b * BLOCK, BLOCK)
                st = nn(jnp.concatenate([kf[ks, :], hot_s[ks, :]], axis=1), qt)
                s_s[r, s * n + b * BLOCK : s * n + (b + 1) * BLOCK, :] = st
                got = jnp.max(group_rows(st), axis=0)
                top = got if top is None else jnp.maximum(top, got)
        tops[r] = jnp.max(top, axis=0, keepdims=True) * (SCALE * LOG2E)

    def soften(r):
        lo, n = SPANS[r]
        cols = slice(r * BLOCK, (r + 1) * BLOCK)
        for s in range(3):
            for t in range(n // TILE):
                e = jnp.exp2(s_s[r, s * n + t * TILE : s * n + (t + 1) * TILE, :] * (SCALE * LOG2E) - tops[r])
                p_s[s, lo + t * TILE : lo + (t + 1) * TILE, cols] = e.astype(BF16)

    tails = {}

    def finish(r):
        lo, n = SPANS[r]
        cols = slice(r * BLOCK, (r + 1) * BLOCK)
        ot = None
        for s in range(3):
            got = nn(vt_s[:, keys(s, lo, n)], p_s[s, lo : lo + n, cols])
            ot = got if ot is None else ot + got
        inv = 1.0 / ot[HD : HD + 1]
        out = (ot[:HD] * inv).astype(BF16)
        of[cols, :] = out.T
        c2 = (ct_s[:HD, cols].astype(F32) * (inv * SCALE)).astype(BF16)
        ct_s[:HD, cols] = c2
        dots = -jnp.sum(c2.astype(F32) * out.astype(F32), axis=0, keepdims=True)
        high = dots.astype(BF16).astype(F32)
        mid = (dots - high).astype(BF16).astype(F32)
        low = dots - high - mid
        shape = (HD, BLOCK)
        tail = marks(shape, 0, 0) * high + marks(shape, 0, 1) * mid + marks(shape, 0, 2) * low
        ct_s[HD:, cols] = tail.astype(BF16)

    unit = (lax.broadcasted_iota(jnp.int32, (BLOCK, HD), 1) < 3).astype(F32).astype(BF16)

    def back(r):
        lo, n = SPANS[r]
        cols = slice(r * BLOCK, (r + 1) * BLOCK)
        c2 = ct_s[:, cols]
        dqt = None
        for s in range(3):
            for b in range(n // BLOCK):
                ks = keys(s, lo + b * BLOCK, BLOCK)
                dp = nn(jnp.concatenate([vf[ks, :], unit], axis=1), c2)
                at = slice(lo + b * BLOCK, lo + (b + 1) * BLOCK)
                d_s[s, at, cols] = p_s[s, at, cols] * dp.astype(BF16)
            got = nn(kt_s[:, keys(s, lo, n)], d_s[s, lo : lo + n, cols])
            dqt = got if dqt is None else dqt + got
        dqf[cols, :] = dqt.astype(BF16).T

    score(0)
    score(1)
    ct_s[:HD, :] = cf[...].T
    vt_s[:HD, :] = vf[...].T
    kt_s[...] = kf[...].T
    soften(0)
    finish(0)
    score(2)
    soften(1)
    finish(1)
    back(0)
    soften(2)
    finish(2)
    back(1)
    back(2)

    outs = []

    def store(src, dst):
        cp = pltpu.make_async_copy(src, dst, out_sems.at[len(outs)])
        cp.start()
        outs.append(cp)

    store(o_s, part(out_ref, frame, 0))
    store(dq_s, part(out_ref, frame, 1))
    for s in (0, 2, 1):
        for a in range(2):
            for b, (lo, n) in enumerate(SPANS):
                at = slice(b * BLOCK, (b + 1) * BLOCK)
                if a == 0:
                    g = nt(qt_s[:HD, lo : lo + n], d_s[s, at, lo : lo + n])
                else:
                    g = nt(ct_s[:HD, lo : lo + n], p_s[s, at, lo : lo + n]) * (1.0 / SCALE)
                g = g.astype(BF16).T
                if edge and s == 2:
                    g = (g.astype(F32) + oldf[a * FRAME + b * BLOCK : a * FRAME + (b + 1) * BLOCK, :].astype(F32)).astype(BF16)
                gf[(a * 3 + s) * FRAME + b * BLOCK : (a * 3 + s) * FRAME + (b + 1) * BLOCK, :] = g
            if s == 1:
                store(gb_s.at[a, s], part(gown_ref, frame, a))
            elif not edge:
                store(gb_s.at[a, s], part(gswap_ref, s // 2, a))
            elif s == 0:
                store(gb_s.at[a, s], gedge_ref.at[:, a])
            else:
                store(gb_s.at[a, s], part(gswap_ref, core, a))
    for cp in outs:
        cp.wait()


def attend(core, mine, swap, bias, edge=None, old=()):
    frame = pltpu.VMEM((CHUNKS, CHUNK, HD), BF16)
    slots = pltpu.VMEM((3, CHUNKS, CHUNK, HD), BF16)
    pair = jax.ShapeDtypeStruct((PLANE, 2, CHUNK, HD), BF16)
    with_edge = edge is not None
    smem, vmem = pl.BlockSpec(memory_space=pltpu.SMEM), pl.BlockSpec(memory_space=pltpu.VMEM)
    edges = (edge,) if with_edge else ()
    shapes = (pair,) * 3 + ((jax.ShapeDtypeStruct((CHUNKS, 2, CHUNK, HD), BF16),) if with_edge else ())
    return pl.pallas_call(
        functools.partial(attend_kernel, with_edge),
        in_specs=[smem, ANY, ANY] + [ANY] * len(edges) + [vmem] + [ANY] * len(old),
        out_specs=(ANY,) * len(shapes),
        out_shape=shapes,
        scratch_shapes=[
            frame,
            frame,
            slots,
            slots,
            pltpu.VMEM((KEYS, HD), BF16),
            pltpu.VMEM((HD, KEYS), BF16),
            pltpu.VMEM((HD + 16, KEYS), BF16),
            pltpu.VMEM((2 * HD, FRAME), BF16),
            pltpu.VMEM((2 * HD, FRAME), BF16),
            pltpu.VMEM((3, 9 * BLOCK, BLOCK), F32),
            pltpu.VMEM((3, FRAME, FRAME), BF16),
            pltpu.VMEM((3, FRAME, FRAME), BF16),
            frame,
            frame,
            pltpu.VMEM((2, 3, CHUNKS, CHUNK, HD), BF16),
            pltpu.VMEM((2, CHUNKS, CHUNK, HD), BF16),
            pltpu.SemaphoreType.DMA((10,)),
            pltpu.SemaphoreType.DMA((8,)),
        ],
        input_output_aliases={5: 0, 6: 1, 7: 2} if with_edge else {},
        name="attend_edge" if with_edge else "attend_local",
    )(core, mine, swap, *edges, bias, *old)


def join_kernel(core_ref, own_ref, swap_ref, edge_ref, out_ref):
    core = core_ref[0]
    for f in range(2):
        here = jnp.where(core == f, 1.0, 0.0)
        for a in range(2):
            for h in range(CHUNKS):
                x = own_ref[f * CHUNKS + h, a].astype(F32) + swap_ref[f * CHUNKS + h, a].astype(F32)
                x = x + edge_ref[h, a].astype(F32) * here
                out_ref[f * CHUNKS + h, a] = x.astype(BF16)


def join(core, own, swap, edge):
    vmem = pl.BlockSpec(memory_space=pltpu.VMEM)
    return pl.pallas_call(
        join_kernel,
        in_specs=[pl.BlockSpec(memory_space=pltpu.SMEM), vmem, vmem, vmem],
        out_specs=vmem,
        out_shape=jax.ShapeDtypeStruct((PLANE, 2, CHUNK, HD), BF16),
        name="join",
    )(core, own, swap, edge)


def tile_bias(neighbours, frame, keyed):
    rows = lax.dynamic_slice_in_dim(neighbours, frame * TILES_F, TILES_F, 0)
    rows = jnp.where(rows >= 0, rows, -2 * TILES_F)
    slot = jnp.arange(HD, dtype=jnp.int32)
    base = sum(jnp.where(slot // TILES_F == i, k, 0) for i, k in enumerate(keyed))
    tiles = base * TILES_F + slot % TILES_F
    hit = jnp.any(rows[None, :, :] == tiles[:, None, None], axis=2)
    return jnp.repeat(jnp.where(hit, 0.0, MASKED).astype(BF16), TILE, axis=1)


def shards(queries, keys, values, cotangent, neighbours):
    plane = ("yl", "head")
    ring = lax.axis_size("sx")
    across = []
    for i in range(ring - 1):
        across.append((2 * i + 1, 2 * i + 2))
        across.append((2 * i + 2, 2 * i + 1))
    swap_pairs = [(0, 1), (1, 0)]
    core = lax.axis_index("co")
    first = 4 * lax.axis_index("sx")
    partner = first + 1 - core
    mid = partner + 2 * core
    bias_local = tile_bias(neighbours, first + 2 - core, (partner, first + 2 - core, partner + 2))
    bias_edge = tile_bias(neighbours, first + 3 * core, (first - 1 + 5 * core, first + 3 * core, mid))
    core_arr = jnp.full((1,), core, jnp.int32)

    mine = lax.all_to_all(pack(queries, keys, values, cotangent), plane, split_axis=0, concat_axis=0, tiled=True)
    kv = mine[:, 1:3]
    swap = lax.ppermute(kv, "co", swap_pairs)
    kv_edge = lax.dynamic_slice_in_dim(kv, core * CHUNKS, CHUNKS, 0)
    edge = lax.ppermute(kv_edge, ("sx", "co"), across)
    done = attend(core_arr, mine, swap, bias_local)
    packed, gown, gswap, gedge = attend(core_arr, mine, swap, bias_edge, edge, done)
    output, grad_query = unpack(lax.all_to_all(packed, plane, split_axis=0, concat_axis=0, tiled=True))
    gswap_in = lax.ppermute(gswap, "co", swap_pairs)
    gedge_in = lax.ppermute(gedge, ("sx", "co"), across)
    gown = join(core_arr, gown, gswap_in, gedge_in)
    grad_key, grad_value = unpack(lax.all_to_all(gown, plane, split_axis=0, concat_axis=0, tiled=True))
    return output, grad_query, grad_key, grad_value


def solution(mesh):
    view = Mesh(mesh.devices.reshape(mesh.devices.shape[0] // 4, 2, 2, -1), ("sx", "yl", "co", "head"))
    rows = P(("sx", "yl", "co", "head"), None)
    return jax.shard_map(
        shards,
        mesh=view,
        in_specs=(rows,) * 4 + (P(),),
        out_specs=(rows,) * 4,
        check_vma=False,
    )
```

```python
import functools
import math

import jax
import jax.numpy as jnp
from jax import lax
from jax.experimental import pallas as pl
from jax.experimental.pallas import tpu as pltpu
from jax.sharding import Mesh, PartitionSpec as P

TILE = 64
TILES_F = 12
HD = 128
FRAME = TILE * TILES_F
BLOCK = 4 * TILE
KEYS = 3 * FRAME
CHUNKS = 8
CHUNK = FRAME // CHUNKS
PLANE = 16
MASKED = -1e30
SCALE = 1.0 / math.sqrt(HD)
LOG2E = 1.4426950408889634
ANY = pl.BlockSpec(memory_space=pl.ANY)
VMEM = pl.BlockSpec(memory_space=pltpu.VMEM)
F32 = jnp.float32
BF16 = jnp.bfloat16


def near(x):
    return pltpu.with_memory_space_constraint(x, pltpu.VMEM)


def far(x):
    return pltpu.with_memory_space_constraint(x, pltpu.HBM)


def enter_kernel(q_ref, k_ref, v_ref, c_ref, near_ref, out_ref, bias_ref, in_s, out_s, in_sem, out_sem):
    ins, outs = [], []
    for a, ref in enumerate((q_ref, k_ref, v_ref, c_ref)):
        ins.append(pltpu.make_async_copy(ref, in_s.at[a], in_sem.at[a]))
        outs.append(pltpu.make_async_copy(out_s.at[a], out_ref.at[:, a], out_sem.at[a]))
        ins[a].start()
    core, first = lax.axis_index("co"), 4 * lax.axis_index("sx")
    partner = first + 1 - core
    local, outer = first + 2 - core, first + 3 * core
    places = (
        (local, (partner, local, partner + 2)),
        (outer, (first - 1 + 5 * core, outer, partner + 2 * core)),
    )
    tiles = near_ref.shape[1]
    slot = lax.broadcasted_iota(jnp.int32, (HD, 1), 0)
    listed = near_ref[...]
    for which, (frame, keyed) in enumerate(places):
        base = jnp.zeros_like(slot)
        for i, k in enumerate(keyed):
            base = jnp.where(slot // TILES_F == i, k, base)
        tile = base * TILES_F + slot % TILES_F
        tile = jnp.where(tile < 0, -TILES_F, tile)
        hit = jnp.zeros((HD, tiles), F32)
        for j in range(listed.shape[0]):
            hit = jnp.where(listed[j : j + 1, :] == tile, 1.0, hit)
        owner = lax.broadcasted_iota(jnp.int32, (tiles, FRAME), 1) // TILE + frame * TILES_F
        spread = (owner == lax.broadcasted_iota(jnp.int32, (tiles, FRAME), 0)).astype(F32).astype(BF16)
        bias_ref[which] = jnp.where(nn(hit.astype(BF16), spread) > 0.5, 0.0, MASKED).astype(BF16)
    for a in range(4):
        ins[a].wait()
        for g in range(PLANE):
            out_s[a, g] = in_s[a, :, g * HD : (g + 1) * HD]
        outs[a].start()
    for cp in outs:
        cp.wait()


def enter(q, k, v, c, neighbours):
    return pl.pallas_call(
        enter_kernel,
        in_specs=[ANY] * 4 + [VMEM],
        out_specs=(ANY, VMEM),
        out_shape=(
            jax.ShapeDtypeStruct((PLANE, 4, CHUNK, HD), BF16),
            jax.ShapeDtypeStruct((2, HD, FRAME), BF16),
        ),
        scratch_shapes=[
            pltpu.VMEM((4, CHUNK, PLANE * HD), BF16),
            pltpu.VMEM((4, PLANE, CHUNK, HD), BF16),
            pltpu.SemaphoreType.DMA((4,)),
            pltpu.SemaphoreType.DMA((4,)),
        ],
        compiler_params=pltpu.CompilerParams(vmem_limit_bytes=32 * 2**20),
        name="enter",
    )(far(q), far(k), far(v), far(c), neighbours.T)


def unpack_kernel(in_ref, *refs):
    sem = refs[-1]
    copies = []
    for a, ref in enumerate(refs[:-1]):
        for g in range(PLANE):
            part = ref.at[:, g * HD : (g + 1) * HD]
            copies.append(pltpu.make_async_copy(in_ref.at[g, a], part, sem.at[a, g]))
    for cp in copies:
        cp.start()
    for cp in copies:
        cp.wait()


def unpack(packed):
    return pl.pallas_call(
        unpack_kernel,
        in_specs=[VMEM],
        out_specs=(ANY,) * 2,
        out_shape=(jax.ShapeDtypeStruct((CHUNK, PLANE * HD), BF16),) * 2,
        scratch_shapes=[pltpu.SemaphoreType.DMA((2, PLANE))],
        name="unpack",
    )(near(packed))


def nt(a, b):
    return lax.dot_general(a, b, (((1,), (1,)), ((), ())), preferred_element_type=F32)


def nn(a, b):
    return lax.dot_general(a, b, (((1,), (0,)), ((), ())), preferred_element_type=F32)


def group_rows(x):
    return x.reshape(x.shape[0] // 8, 8, x.shape[1])


def marks(shape, dim, row):
    return (lax.broadcasted_iota(jnp.int32, shape, dim) == row).astype(F32)


SPANS = ((0, 2 * BLOCK), (0, 3 * BLOCK), (BLOCK, 2 * BLOCK))


def attend_kernel(edge, *refs):
    refs = list(refs)
    mine_ref, swap_ref = refs[:2]
    del refs[:2]
    edge_ref = refs.pop(0) if edge else None
    bias_ref = refs.pop(0)
    old_refs = refs[:3] if edge else None
    if edge:
        del refs[:3]
    out_ref, gown_ref, gswap_ref = refs[:3]
    del refs[:3]
    gedge_ref = refs.pop(0) if edge else None
    (q_s, c_s, k_s, v_s, hot_s, kt_s, vt_s, qt_s, ct_s, s_s, p_s, d_s, o_s, dq_s, gb_s) = refs

    core = lax.axis_index("co")
    frame = core if edge else 1 - core

    for h in range(CHUNKS):
        q_s[h] = mine_ref[frame * CHUNKS + h, 0]
    for a, dst in ((0, k_s), (1, v_s)):
        for h in range(CHUNKS):
            if edge:
                dst[0, h] = edge_ref[h, a]
                dst[2, h] = swap_ref[core * CHUNKS + h, a]
            else:
                dst[0, h] = swap_ref[h, a]
                dst[2, h] = swap_ref[CHUNKS + h, a]
            dst[1, h] = mine_ref[frame * CHUNKS + h, 1 + a]
    for h in range(CHUNKS):
        c_s[h] = mine_ref[frame * CHUNKS + h, 3]

    lane = lax.broadcasted_iota(jnp.int32, (TILE, HD), 1)
    for t in range(3 * TILES_F):
        hot_s[t * TILE : (t + 1) * TILE, :] = (lane == t).astype(F32).astype(BF16)
    qt_s[HD:, :] = bias_ref[1 if edge else 0]
    vt_s[HD:, :] = marks((16, KEYS), 0, 0).astype(BF16)

    qf = q_s.reshape(FRAME, HD)
    cf = c_s.reshape(FRAME, HD)
    kf = k_s.reshape(KEYS, HD)
    vf = v_s.reshape(KEYS, HD)
    of = o_s.reshape(FRAME, HD)
    dqf = dq_s.reshape(FRAME, HD)
    gf = gb_s.reshape(2 * KEYS, HD)

    qt_s[:HD, :] = qf[...].T

    def keys(s, lo, n):
        return slice(s * FRAME + lo, s * FRAME + lo + n)

    tops = {}

    def score(r):
        lo, n = SPANS[r]
        cols = slice(r * BLOCK, (r + 1) * BLOCK)
        qt = qt_s[:, cols]
        top = None
        for s in range(3):
            for b in range(n // BLOCK):
                ks = keys(s, lo + b * BLOCK, BLOCK)
                st = nn(jnp.concatenate([kf[ks, :], hot_s[ks, :]], axis=1), qt)
                s_s[r, s * n + b * BLOCK : s * n + (b + 1) * BLOCK, :] = st
                got = jnp.max(group_rows(st), axis=0)
                top = got if top is None else jnp.maximum(top, got)
        tops[r] = jnp.max(top, axis=0, keepdims=True) * (SCALE * LOG2E)

    def soften(r):
        lo, n = SPANS[r]
        cols = slice(r * BLOCK, (r + 1) * BLOCK)
        for s in range(3):
            for t in range(n // TILE):
                e = jnp.exp2(s_s[r, s * n + t * TILE : s * n + (t + 1) * TILE, :] * (SCALE * LOG2E) - tops[r])
                p_s[s, lo + t * TILE : lo + (t + 1) * TILE, cols] = e.astype(BF16)

    tails = {}

    def finish(r):
        lo, n = SPANS[r]
        cols = slice(r * BLOCK, (r + 1) * BLOCK)
        ot = None
        for s in range(3):
            got = nn(vt_s[:, keys(s, lo, n)], p_s[s, lo : lo + n, cols])
            ot = got if ot is None else ot + got
        inv = 1.0 / ot[HD : HD + 1]
        out = (ot[:HD] * inv).astype(BF16)
        of[cols, :] = out.T
        c2 = (ct_s[:HD, cols].astype(F32) * (inv * SCALE)).astype(BF16)
        ct_s[:HD, cols] = c2
        dots = -jnp.sum(c2.astype(F32) * out.astype(F32), axis=0, keepdims=True)
        high = dots.astype(BF16).astype(F32)
        mid = (dots - high).astype(BF16).astype(F32)
        low = dots - high - mid
        shape = (HD, BLOCK)
        tail = marks(shape, 0, 0) * high + marks(shape, 0, 1) * mid + marks(shape, 0, 2) * low
        ct_s[HD:, cols] = tail.astype(BF16)

    unit = (lax.broadcasted_iota(jnp.int32, (BLOCK, HD), 1) < 3).astype(F32).astype(BF16)

    def back(r):
        lo, n = SPANS[r]
        cols = slice(r * BLOCK, (r + 1) * BLOCK)
        c2 = ct_s[:, cols]
        dqt = None
        for s in range(3):
            for b in range(n // BLOCK):
                ks = keys(s, lo + b * BLOCK, BLOCK)
                dp = nn(jnp.concatenate([vf[ks, :], unit], axis=1), c2)
                at = slice(lo + b * BLOCK, lo + (b + 1) * BLOCK)
                d_s[s, at, cols] = p_s[s, at, cols] * dp.astype(BF16)
            got = nn(kt_s[:, keys(s, lo, n)], d_s[s, lo : lo + n, cols])
            dqt = got if dqt is None else dqt + got
        dqf[cols, :] = dqt.astype(BF16).T

    score(0)
    score(1)
    ct_s[:HD, :] = cf[...].T
    vt_s[:HD, :] = vf[...].T
    kt_s[...] = kf[...].T
    soften(0)
    finish(0)
    score(2)
    soften(1)
    finish(1)
    back(0)
    soften(2)
    finish(2)
    back(1)
    back(2)

    place = frame if edge else 0

    def store(src, ref, index, a):
        for h in range(CHUNKS):
            ref[index * CHUNKS + h, a] = src[h]

    if edge:
        other = 1 - core
        for old, new in zip(old_refs[:2], (out_ref, gown_ref)):
            for a in range(2):
                for h in range(CHUNKS):
                    new[other * CHUNKS + h, a] = old[h, a]
        for a in range(2):
            for h in range(CHUNKS):
                gswap_ref[other * CHUNKS + h, a] = old_refs[2][other * CHUNKS + h, a]
    store(o_s, out_ref, place, 0)
    store(dq_s, out_ref, place, 1)
    for s in (0, 2, 1):
        for a in range(2):
            for b, (lo, n) in enumerate(SPANS):
                at = slice(b * BLOCK, (b + 1) * BLOCK)
                if a == 0:
                    g = nt(qt_s[:HD, lo : lo + n], d_s[s, at, lo : lo + n])
                else:
                    g = nt(ct_s[:HD, lo : lo + n], p_s[s, at, lo : lo + n]) * (1.0 / SCALE)
                row = (a * 3 + s) * FRAME + b * BLOCK
                gf[row : row + BLOCK, :] = g.astype(BF16).T
            if s == 1:
                store(gb_s.at[a, s], gown_ref, place, a)
            elif not edge:
                store(gb_s.at[a, s], gswap_ref, s // 2, a)
            elif s == 0:
                store(gb_s.at[a, s], gedge_ref, 0, a)
            else:
                for h in range(CHUNKS):
                    both = gb_s[a, s, h].astype(F32) + old_refs[2][core * CHUNKS + h, a].astype(F32)
                    gswap_ref[core * CHUNKS + h, a] = both.astype(BF16)


def attend(mine, swap, bias, edge=None, old=()):
    frame = pltpu.VMEM((CHUNKS, CHUNK, HD), BF16)
    slots = pltpu.VMEM((3, CHUNKS, CHUNK, HD), BF16)
    pair = jax.ShapeDtypeStruct((PLANE, 2, CHUNK, HD), BF16)
    half = jax.ShapeDtypeStruct((CHUNKS, 2, CHUNK, HD), BF16)
    out = pltpu.HBM((PLANE, 2, CHUNK, HD), BF16)
    with_edge = edge is not None
    edges = (near(edge),) if with_edge else ()
    shapes = (out, out, pair, half) if with_edge else (half, half, pair)
    return pl.pallas_call(
        functools.partial(attend_kernel, with_edge),
        in_specs=[VMEM, VMEM] + [VMEM] * len(edges) + [VMEM] + [VMEM] * len(old),
        out_specs=(VMEM,) * len(shapes),
        out_shape=shapes,
        scratch_shapes=[
            frame,
            frame,
            slots,
            slots,
            pltpu.VMEM((KEYS, HD), BF16),
            pltpu.VMEM((HD, KEYS), BF16),
            pltpu.VMEM((HD + 16, KEYS), BF16),
            pltpu.VMEM((2 * HD, FRAME), BF16),
            pltpu.VMEM((2 * HD, FRAME), BF16),
            pltpu.VMEM((3, 9 * BLOCK, BLOCK), F32),
            pltpu.VMEM((3, FRAME, FRAME), BF16),
            pltpu.VMEM((3, FRAME, FRAME), BF16),
            frame,
            frame,
            pltpu.VMEM((2, 3, CHUNKS, CHUNK, HD), BF16),
        ],
        compiler_params=pltpu.CompilerParams(vmem_limit_bytes=32 * 2**20),
        name="attend_edge" if with_edge else "attend_local",
    )(near(mine), near(swap), *edges, bias, *old)


def join_kernel(own_ref, swap_ref, edge_ref, out_ref):
    core = lax.axis_index("co")
    for f in range(2):
        here = jnp.where(core == f, 1.0, 0.0)
        for a in range(2):
            for h in range(CHUNKS):
                x = own_ref[f * CHUNKS + h, a].astype(F32) + swap_ref[f * CHUNKS + h, a].astype(F32)
                x = x + edge_ref[h, a].astype(F32) * here
                out_ref[f * CHUNKS + h, a] = x.astype(BF16)


def join(own, swap, edge):
    return pl.pallas_call(
        join_kernel,
        in_specs=[VMEM, VMEM, VMEM],
        out_specs=VMEM,
        out_shape=jax.ShapeDtypeStruct((PLANE, 2, CHUNK, HD), BF16),
        name="join",
    )(own, near(swap), near(edge))


def shards(queries, keys, values, cotangent, neighbours):
    plane = ("yl", "head")
    ring = lax.axis_size("sx")
    across = []
    for i in range(ring - 1):
        across.append((2 * i + 1, 2 * i + 2))
        across.append((2 * i + 2, 2 * i + 1))
    swap_pairs = [(0, 1), (1, 0)]
    core = lax.axis_index("co")
    sent, bias = enter(queries, keys, values, cotangent, neighbours)
    with jax.named_scope("enter_all"):
        mine = lax.all_to_all(sent, plane, split_axis=0, concat_axis=0, tiled=True)
    kv = mine[:, 1:3]
    swap = lax.ppermute(kv, "co", swap_pairs)
    kv_edge = lax.dynamic_slice_in_dim(kv, core * CHUNKS, CHUNKS, 0)
    edge = lax.ppermute(kv_edge, ("sx", "co"), across)
    done = attend(mine, swap, bias)
    packed, gown, gswap, gedge = attend(mine, swap, bias, edge, done)
    output, grad_query = unpack(lax.all_to_all(packed, plane, split_axis=0, concat_axis=0, tiled=True))
    gswap_in = lax.ppermute(gswap, "co", swap_pairs)
    gedge_in = lax.ppermute(gedge, ("sx", "co"), across)
    gown = join(gown, gswap_in, gedge_in)
    grad_key, grad_value = unpack(lax.all_to_all(gown, plane, split_axis=0, concat_axis=0, tiled=True))
    return output, grad_query, grad_key, grad_value


def solution(mesh):
    view = Mesh(mesh.devices.reshape(mesh.devices.shape[0] // 4, 2, 2, -1), ("sx", "yl", "co", "head"))
    rows = P(("sx", "yl", "co", "head"), None)
    return jax.shard_map(
        shards,
        mesh=view,
        in_specs=(rows,) * 4 + (P(),),
        out_specs=(rows,) * 4,
        check_vma=False,
    )
```

```python
import math

import jax
import jax.numpy as jnp
from jax import lax
from jax.experimental import pallas as pl
from jax.experimental.pallas import tpu as pltpu
from jax.sharding import Mesh, PartitionSpec as P


TILE = 64
TILES_F = 12
HD = 128
FRAME = TILE * TILES_F
BLOCK = 4 * TILE
KEYS = 3 * FRAME
CHUNKS = 8
CHUNK = FRAME // CHUNKS
PLANE = 16
MASKED = -1e30
SCALE = 1.0 / math.sqrt(HD)
LOG2E = 1.4426950408889634
ANY = pl.BlockSpec(memory_space=pl.ANY)
VMEM = pl.BlockSpec(memory_space=pltpu.VMEM)
F32 = jnp.float32
BF16 = jnp.bfloat16


def near(x):
    return pltpu.with_memory_space_constraint(x, pltpu.VMEM)


def far(x):
    return pltpu.with_memory_space_constraint(x, pltpu.HBM)


def room(mib):
    return pltpu.CompilerParams(vmem_limit_bytes=mib * 2**20)


def enter_kernel(q_ref, k_ref, v_ref, c_ref, near_ref, out_ref, bias_ref, near_s, in_s, out_s, in_sem, out_sem):
    listing = pltpu.make_async_copy(near_ref, near_s, in_sem.at[4])
    listing.start()
    ins, outs = [], []
    for a, ref in enumerate((q_ref, k_ref, v_ref, c_ref)):
        ins.append(pltpu.make_async_copy(ref, in_s.at[a], in_sem.at[a]))
        outs.append(pltpu.make_async_copy(out_s.at[a], out_ref.at[:, a], out_sem.at[a]))
        ins[a].start()
    core, first = lax.axis_index("co"), 4 * lax.axis_index("sx")
    partner = first + 1 - core
    local, outer = first + 2 - core, first + 3 * core
    places = (
        (local, (partner, local, partner + 2)),
        (outer, (first - 1 + 5 * core, outer, partner + 2 * core)),
    )
    tiles = near_ref.shape[1]
    slot = lax.broadcasted_iota(jnp.int32, (HD, 1), 0)
    listing.wait()
    listed = near_s[...]
    for which, (frame, keyed) in enumerate(places):
        base = jnp.zeros_like(slot)
        for i, k in enumerate(keyed):
            base = jnp.where(slot // TILES_F == i, k, base)
        tile = base * TILES_F + slot % TILES_F
        tile = jnp.where(tile < 0, -TILES_F, tile)
        hit = jnp.zeros((HD, tiles), F32)
        for j in range(listed.shape[0]):
            hit = jnp.where(listed[j : j + 1, :] == tile, 1.0, hit)
        owner = lax.broadcasted_iota(jnp.int32, (tiles, FRAME), 1) // TILE + frame * TILES_F
        spread = (owner == lax.broadcasted_iota(jnp.int32, (tiles, FRAME), 0)).astype(F32).astype(BF16)
        bias_ref[which] = jnp.where(nn(hit.astype(BF16), spread) > 0.5, 0.0, MASKED).astype(BF16)
    for a in range(4):
        ins[a].wait()
        for g in range(PLANE):
            out_s[a, g] = in_s[a, :, g * HD : (g + 1) * HD]
        outs[a].start()
    for cp in outs:
        cp.wait()


def enter(q, k, v, c, neighbours):
    return pl.pallas_call(
        enter_kernel,
        in_specs=[ANY] * 5,
        out_specs=(ANY, VMEM),
        out_shape=(
            jax.ShapeDtypeStruct((PLANE, 4, CHUNK, HD), BF16),
            jax.ShapeDtypeStruct((2, HD, FRAME), BF16),
        ),
        scratch_shapes=[
            pltpu.VMEM(neighbours.shape[::-1], jnp.int32),
            pltpu.VMEM((4, CHUNK, PLANE * HD), BF16),
            pltpu.VMEM((4, PLANE, CHUNK, HD), BF16),
            pltpu.SemaphoreType.DMA((5,)),
            pltpu.SemaphoreType.DMA((4,)),
        ],
        compiler_params=room(12),
        name="enter",
    )(far(q), far(k), far(v), far(c), far(neighbours.T))


def unpack_kernel(in_ref, *refs):
    sem = refs[-1]
    copies = []
    for a, ref in enumerate(refs[:-1]):
        for g in range(PLANE):
            part = ref.at[:, g * HD : (g + 1) * HD]
            copies.append(pltpu.make_async_copy(in_ref.at[g, a], part, sem.at[a, g]))
    for cp in copies:
        cp.start()
    for cp in copies:
        cp.wait()


def unpack(packed):
    return pl.pallas_call(
        unpack_kernel,
        in_specs=[VMEM],
        out_specs=(ANY,) * 4,
        out_shape=(jax.ShapeDtypeStruct((CHUNK, PLANE * HD), BF16),) * 4,
        scratch_shapes=[pltpu.SemaphoreType.DMA((4, PLANE))],
        compiler_params=room(4),
        name="unpack",
    )(near(packed))


def nt(a, b):
    return lax.dot_general(a, b, (((1,), (1,)), ((), ())), preferred_element_type=F32)


def nn(a, b):
    return lax.dot_general(a, b, (((1,), (0,)), ((), ())), preferred_element_type=F32)


def group_rows(x):
    return x.reshape(x.shape[0] // 8, 8, x.shape[1])


def marks(shape, dim, row):
    return (lax.broadcasted_iota(jnp.int32, shape, dim) == row).astype(F32)


SPANS = ((0, 2 * BLOCK), (0, 3 * BLOCK), (BLOCK, 2 * BLOCK))


def tokens(ref):
    return ref.reshape(ref.shape[0] * ref.shape[1], HD)


def keys(s, lo, n):
    return slice(s * FRAME + lo, s * FRAME + lo + n)


def block(r):
    return slice(r * BLOCK, (r + 1) * BLOCK)


def fetch(ref, index, a, dst):
    for h in range(CHUNKS):
        dst[h] = ref[index * CHUNKS + h, a]


def put(src, ref, index, a):
    for h in range(CHUNKS):
        ref[index * CHUNKS + h, a] = src[h]


class Scores:
    def __init__(self, k, hot, vt, qt, ct, c2, s, p, out):
        self.k, self.hot, self.vt, self.qt, self.ct, self.c2, self.s, self.p, self.out = k, hot, vt, qt, ct, c2, s, p, out
        self.tops, self.sums = {}, {}
        lane = lax.broadcasted_iota(jnp.int32, (TILE, HD), 1)
        for t in range(3 * TILES_F):
            hot[t * TILE : (t + 1) * TILE, :] = (lane == t).astype(F32).astype(BF16)
        vt[HD:, :] = marks((16, KEYS), 0, 0).astype(BF16)

    def score(self, r, s):
        lo, n = SPANS[r]
        kf = tokens(self.k)
        qt = self.qt[:, block(r)]
        for b in range(n // BLOCK):
            ks = keys(s, lo + b * BLOCK, BLOCK)
            st = nn(jnp.concatenate([kf[ks, :], self.hot[ks, :]], axis=1), qt)
            self.s[r, s * n + b * BLOCK : s * n + (b + 1) * BLOCK, :] = st
            got = jnp.max(group_rows(st), axis=0)
            self.tops[r] = jnp.maximum(self.tops[r], got) if r in self.tops else got
        if s == 2:
            self.tops[r] = jnp.max(self.tops[r], axis=0, keepdims=True) * (SCALE * LOG2E)

    def soften(self, r, s):
        lo, n = SPANS[r]
        for t in range(n // TILE):
            x = self.s[r, s * n + t * TILE : s * n + (t + 1) * TILE, :]
            e = jnp.exp2(x * (SCALE * LOG2E) - self.tops[r])
            self.p[s][lo + t * TILE : lo + (t + 1) * TILE, block(r)] = e.astype(BF16)
        got = nn(self.vt[:, keys(s, lo, n)], self.p[s][lo : lo + n, block(r)])
        self.sums[r] = self.sums[r] + got if r in self.sums else got

    def finish(self, r):
        cols = block(r)
        ot = self.sums[r]
        inv = 1.0 / ot[HD : HD + 1]
        out = (ot[:HD] * inv).astype(BF16)
        tokens(self.out)[cols, :] = out.T
        c2 = (self.ct[:, cols].astype(F32) * (inv * SCALE)).astype(BF16)
        self.c2[:HD, cols] = c2
        dots = -jnp.sum(c2.astype(F32) * out.astype(F32), axis=0, keepdims=True)
        high = dots.astype(BF16).astype(F32)
        mid = (dots - high).astype(BF16).astype(F32)
        low = dots - high - mid
        shape = (HD, BLOCK)
        tail = marks(shape, 0, 0) * high + marks(shape, 0, 1) * mid + marks(shape, 0, 2) * low
        self.c2[HD:, cols] = tail.astype(BF16)


class Grads:
    def __init__(self, v, kt, qt, c2, p, d):
        self.v, self.kt, self.qt, self.c2, self.p, self.d = v, kt, qt, c2, p, d
        self.sums = {}
        self.unit = (lax.broadcasted_iota(jnp.int32, (BLOCK, HD), 1) < 3).astype(F32).astype(BF16)

    def back(self, r, s):
        lo, n = SPANS[r]
        cols = block(r)
        vf = tokens(self.v)
        for b in range(n // BLOCK):
            at = slice(lo + b * BLOCK, lo + (b + 1) * BLOCK)
            rows = jnp.concatenate([vf[keys(s, lo + b * BLOCK, BLOCK), :], self.unit], axis=1)
            dp = nn(rows, self.c2[:, cols])
            self.d[s][at, cols] = self.p[s][at, cols] * dp.astype(BF16)
        got = nn(self.kt[:, keys(s, lo, n)], self.d[s][lo : lo + n, cols])
        self.sums[r] = self.sums[r] + got if r in self.sums else got

    def keyed(self, s, a):
        for b, (lo, n) in enumerate(SPANS):
            if a == 0:
                g = nt(self.qt[:HD, lo : lo + n], self.d[s][block(b), lo : lo + n])
            else:
                g = nt(self.c2[:HD, lo : lo + n], self.p[s][block(b), lo : lo + n]) * (1.0 / SCALE)
            yield block(b), g.astype(BF16).T


def run_scores(sc, ready):
    for s in range(3):
        sc.score(0, s)
    ready()
    for s in range(3):
        sc.score(1, s)
        sc.soften(0, s)
    sc.finish(0)
    for s in range(3):
        sc.score(2, s)
        sc.soften(1, s)
    sc.finish(1)


def local_kernel(
    mine_ref, swap_ref, bias_ref, out_ref, gown_ref, gswap_ref,
    q_s, c_s, o_s, g_s, k_s, v_s, hot_s, kt_s, vt_s, qt_s, ct_s, c2_s, s_s, p_s, d_s,
):
    frame = 1 - lax.axis_index("co")
    fetch(mine_ref, frame, 0, q_s)
    for a, dst in ((0, k_s), (1, v_s)):
        for s in range(3):
            for h in range(CHUNKS):
                dst[s * CHUNKS + h] = mine_ref[frame * CHUNKS + h, 1 + a] if s == 1 else swap_ref[s // 2 * CHUNKS + h, a]
    fetch(mine_ref, frame, 3, c_s)
    qt_s[:HD, :] = tokens(q_s)[...].T
    qt_s[HD:, :] = bias_ref[0]
    ps, ds = [p_s.at[s] for s in range(3)], [d_s.at[s] for s in range(3)]
    sc = Scores(k_s, hot_s, vt_s, qt_s, ct_s, c2_s, s_s, ps, o_s)
    gr = Grads(v_s, kt_s, qt_s, c2_s, ps, ds)

    def ready():
        vt_s[:HD, :] = tokens(v_s)[...].T
        ct_s[...] = tokens(c_s)[...].T

    run_scores(sc, ready)
    kt_s[...] = tokens(k_s)[...].T
    for s in range(3):
        gr.back(0, s)
        sc.soften(2, s)
    sc.finish(2)
    for s in range(3):
        gr.back(1, s)
        gr.back(2, s)
    for r in range(3):
        tokens(q_s)[block(r), :] = gr.sums[r].astype(BF16).T
    put(o_s, out_ref, 0, 0)
    put(q_s, out_ref, 0, 1)
    for s in (0, 2, 1):
        for a in range(2):
            for rows, g in gr.keyed(s, a):
                tokens(g_s.at[a, s])[rows, :] = g
            if s == 1:
                put(g_s.at[a, s], gown_ref, 0, a)
            else:
                put(g_s.at[a, s], gswap_ref, s // 2, a)


def outer_kernel(
    mine_ref, swap_ref, edge_ref, bias_ref, out_ref, p_ref, qt_ref, c2_ref, dqt_ref, gedge_ref,
    q_s, c_s, o_s, g_s, k_s, v_s, hot_s, kt_s, vt_s, ct_s, s_s, p_s, d_s,
):
    core = lax.axis_index("co")
    fetch(mine_ref, core, 0, q_s)
    for a, dst in ((0, k_s), (1, v_s)):
        for h in range(CHUNKS):
            dst[h] = edge_ref[h, a]
            dst[CHUNKS + h] = mine_ref[core * CHUNKS + h, 1 + a]
            dst[2 * CHUNKS + h] = swap_ref[core * CHUNKS + h, a]
    fetch(mine_ref, core, 3, c_s)
    qt_ref[:HD, :] = tokens(q_s)[...].T
    qt_ref[HD:, :] = bias_ref[1]
    ps = [p_s, p_ref.at[0], p_ref.at[1]]
    sc = Scores(k_s, hot_s, vt_s, qt_ref, ct_s, c2_ref, s_s, ps, o_s)
    gr = Grads(v_s, kt_s, qt_ref, c2_ref, ps, [d_s])

    def ready():
        vt_s[:HD, :] = tokens(v_s)[...].T
        ct_s[...] = tokens(c_s)[...].T

    run_scores(sc, ready)
    kt_s[...] = tokens(k_s)[:FRAME, :].T
    gr.back(0, 0)
    for s in range(3):
        sc.soften(2, s)
    sc.finish(2)
    gr.back(1, 0)
    gr.back(2, 0)
    for r in range(3):
        dqt_ref[:, block(r)] = gr.sums[r]
    put(o_s, out_ref, 0, 0)
    for a in range(2):
        for rows, g in gr.keyed(0, a):
            tokens(g_s.at[a])[rows, :] = g
        put(g_s.at[a], gedge_ref, 0, a)


def inner_kernel(
    mine_ref, swap_ref, p_ref, qt_ref, c2_ref, dqt_ref, old_ref, dq_ref, gown_ref, gswap_ref,
    g_s, k_s, v_s, kt_s, d_s,
):
    core = lax.axis_index("co")
    for a, dst in ((0, k_s), (1, v_s)):
        for h in range(CHUNKS):
            dst[h] = mine_ref[core * CHUNKS + h, 1 + a]
            dst[CHUNKS + h] = swap_ref[core * CHUNKS + h, a]
    gr = Grads(v_s, kt_s, qt_ref, c2_ref, [p_ref.at[s] for s in range(2)], [d_s.at[s] for s in range(2)])
    kt_s[...] = tokens(k_s)[...].T
    for r in range(3):
        for s in range(2):
            gr.back(r, s)
    for r in range(3):
        tokens(g_s.at[0, 0])[block(r), :] = (gr.sums[r] + dqt_ref[:, block(r)]).astype(BF16).T
    for h in range(CHUNKS):
        dq_ref[h] = g_s[0, 0, h]
    for s in (1, 0):
        for a in range(2):
            for rows, g in gr.keyed(s, a):
                tokens(g_s.at[a, s])[rows, :] = g
            for h in range(CHUNKS):
                if s == 0:
                    gown_ref[h, a] = g_s[a, s, h]
                else:
                    both = g_s[a, s, h].astype(F32) + old_ref[core * CHUNKS + h, a].astype(F32)
                    gswap_ref[core * CHUNKS + h, a] = both.astype(BF16)
                    gswap_ref[(1 - core) * CHUNKS + h, a] = old_ref[(1 - core) * CHUNKS + h, a]


PAIR = jax.ShapeDtypeStruct((PLANE, 2, CHUNK, HD), BF16)
HALF = jax.ShapeDtypeStruct((CHUNKS, 2, CHUNK, HD), BF16)
ONE = jax.ShapeDtypeStruct((CHUNKS, CHUNK, HD), BF16)


def frames(*shape):
    return pltpu.VMEM((*shape, CHUNK, HD), BF16)


def wide(rows):
    return pltpu.VMEM((rows, FRAME), BF16)


def attend_local(mine, swap, bias):
    square = pltpu.VMEM((3, FRAME, FRAME), BF16)
    return pl.pallas_call(
        local_kernel,
        in_specs=[VMEM] * 3,
        out_specs=(VMEM,) * 3,
        out_shape=(HALF, HALF, PAIR),
        scratch_shapes=[
            frames(CHUNKS),
            frames(CHUNKS),
            frames(CHUNKS),
            frames(2, 3, CHUNKS),
            frames(3 * CHUNKS),
            frames(3 * CHUNKS),
            pltpu.VMEM((KEYS, HD), BF16),
            pltpu.VMEM((HD, KEYS), BF16),
            pltpu.VMEM((HD + 16, KEYS), BF16),
            wide(2 * HD),
            wide(HD),
            wide(2 * HD),
            pltpu.VMEM((3, 9 * BLOCK, BLOCK), F32),
            square,
            square,
        ],
        compiler_params=room(26),
        name="attend_local",
    )(near(mine), near(swap), bias)


def attend_outer(mine, swap, edge, bias):
    return pl.pallas_call(
        outer_kernel,
        in_specs=[VMEM] * 4,
        out_specs=(VMEM,) * 6,
        out_shape=(
            jax.ShapeDtypeStruct((CHUNKS, 1, CHUNK, HD), BF16),
            jax.ShapeDtypeStruct((2, FRAME, FRAME), BF16),
            jax.ShapeDtypeStruct((2 * HD, FRAME), BF16),
            jax.ShapeDtypeStruct((2 * HD, FRAME), BF16),
            jax.ShapeDtypeStruct((HD, FRAME), F32),
            HALF,
        ),
        scratch_shapes=[
            frames(CHUNKS),
            frames(CHUNKS),
            frames(CHUNKS),
            frames(2, CHUNKS),
            frames(3 * CHUNKS),
            frames(3 * CHUNKS),
            pltpu.VMEM((KEYS, HD), BF16),
            wide(HD),
            pltpu.VMEM((HD + 16, KEYS), BF16),
            wide(HD),
            pltpu.VMEM((3, 9 * BLOCK, BLOCK), F32),
            wide(FRAME),
            wide(FRAME),
        ],
        compiler_params=room(26),
        name="attend_outer",
    )(near(mine), near(swap), near(edge), bias)


def attend_inner(mine, swap, p, qt, c2, dqt, old):
    return pl.pallas_call(
        inner_kernel,
        in_specs=[VMEM] * 7,
        out_specs=(VMEM,) * 3,
        out_shape=(ONE, HALF, PAIR),
        scratch_shapes=[
            frames(2, 2, CHUNKS),
            frames(2 * CHUNKS),
            frames(2 * CHUNKS),
            pltpu.VMEM((HD, 2 * FRAME), BF16),
            pltpu.VMEM((2, FRAME, FRAME), BF16),
        ],
        compiler_params=room(14),
        name="attend_inner",
    )(near(mine), near(swap), p, qt, c2, dqt, old)


def join_kernel(local_ref, outer_ref, dq_ref, lown_ref, eown_ref, swap_ref, edge_ref, out_ref):
    core = lax.axis_index("co")
    for h in range(CHUNKS):
        here, there = core * CHUNKS + h, (1 - core) * CHUNKS + h
        out_ref[there, 0] = local_ref[h, 0]
        out_ref[there, 1] = local_ref[h, 1]
        out_ref[here, 0] = outer_ref[h, 0]
        out_ref[here, 1] = dq_ref[h]
        for a in range(2):
            x = lown_ref[h, a].astype(F32) + swap_ref[there, a].astype(F32)
            out_ref[there, 2 + a] = x.astype(BF16)
            x = eown_ref[h, a].astype(F32) + swap_ref[here, a].astype(F32)
            out_ref[here, 2 + a] = (x + edge_ref[h, a].astype(F32)).astype(BF16)


def join(*parts):
    swap, edge = parts[-2:]
    return pl.pallas_call(
        join_kernel,
        in_specs=[VMEM] * 7,
        out_specs=VMEM,
        out_shape=jax.ShapeDtypeStruct((PLANE, 4, CHUNK, HD), BF16),
        compiler_params=room(10),
        name="join",
    )(*parts[:-2], near(swap), near(edge))


def shards(queries, keys, values, cotangent, neighbours):
    plane = ("yl", "head")
    ring = lax.axis_size("sx")
    across = []
    for i in range(ring - 1):
        across.append((2 * i + 1, 2 * i + 2))
        across.append((2 * i + 2, 2 * i + 1))
    swap_pairs = [(0, 1), (1, 0)]
    core = lax.axis_index("co")
    sent, bias = enter(queries, keys, values, cotangent, neighbours)
    mine = lax.all_to_all(sent, plane, split_axis=0, concat_axis=0, tiled=True)
    kv = mine[:, 1:3]
    swap = lax.ppermute(kv, "co", swap_pairs)
    kv_edge = lax.dynamic_slice_in_dim(kv, core * CHUNKS, CHUNKS, 0)
    edge = lax.ppermute(kv_edge, ("sx", "co"), across)
    local, lown, lswap = attend_local(mine, swap, bias)
    outer, *kept, gedge = attend_outer(mine, swap, edge, bias)
    gedge_in = lax.ppermute(gedge, ("sx", "co"), across)
    dq, eown, gswap = attend_inner(mine, swap, *kept, lswap)
    gswap_in = lax.ppermute(gswap, "co", swap_pairs)
    packed = join(local, outer, dq, lown, eown, gswap_in, gedge_in)
    return unpack(lax.all_to_all(packed, plane, split_axis=0, concat_axis=0, tiled=True))


def solution(mesh):
    view = Mesh(mesh.devices.reshape(mesh.devices.shape[0] // 4, 2, 2, -1), ("sx", "yl", "co", "head"))
    rows = P(("sx", "yl", "co", "head"), None)
    return jax.shard_map(
        shards,
        mesh=view,
        in_specs=(rows,) * 4 + (P(),),
        out_specs=(rows,) * 4,
        check_vma=False,
    )
```

```python
import math

import jax
import jax.numpy as jnp
from jax import lax
from jax.experimental import pallas as pl
from jax.experimental.pallas import tpu as pltpu
from jax.sharding import Mesh, PartitionSpec as P


TILE = 64
TILES_F = 12
HD = 128
FRAME = TILE * TILES_F
BLOCK = 4 * TILE
KEYS = 3 * FRAME
CHUNKS = 8
CHUNK = FRAME // CHUNKS
PLANE = 16
MASKED = -1e30
SCALE = 1.0 / math.sqrt(HD)
LOG2E = 1.4426950408889634
ANY = pl.BlockSpec(memory_space=pl.ANY)
VMEM = pl.BlockSpec(memory_space=pltpu.VMEM)
F32 = jnp.float32
BF16 = jnp.bfloat16


def near(x):
    return pltpu.with_memory_space_constraint(x, pltpu.VMEM)


def far(x):
    return pltpu.with_memory_space_constraint(x, pltpu.HBM)


def room(mib):
    return pltpu.CompilerParams(vmem_limit_bytes=mib * 2**20)


def enter_kernel(q_ref, k_ref, v_ref, c_ref, out_ref, in_s, in_sem):
    ins = []
    for a, ref in enumerate((q_ref, k_ref, v_ref, c_ref)):
        ins.append(pltpu.make_async_copy(ref, in_s.at[a], in_sem.at[a]))
        ins[a].start()
    for a in range(4):
        ins[a].wait()
        for g in range(PLANE):
            out_ref[g, a] = in_s[a, :, g * HD : (g + 1) * HD]


def enter(*parts):
    return pl.pallas_call(
        enter_kernel,
        in_specs=[ANY] * 4,
        out_specs=VMEM,
        out_shape=jax.ShapeDtypeStruct((PLANE, 4, CHUNK, HD), BF16),
        scratch_shapes=[pltpu.VMEM((4, CHUNK, PLANE * HD), BF16), pltpu.SemaphoreType.DMA((4,))],
        compiler_params=room(8),
        name="enter",
    )(*(far(x) for x in parts))


def unpack_kernel(in_ref, *refs):
    outs, (rows_s, sem) = refs[:-2], refs[-2:]
    copies = []
    for a, ref in enumerate(outs):
        for g in range(PLANE):
            rows_s[a, :, g * HD : (g + 1) * HD] = in_ref[g, a]
        copies.append(pltpu.make_async_copy(rows_s.at[a], ref, sem.at[a]))
        copies[a].start()
    for cp in copies:
        cp.wait()


def unpack(packed):
    return pl.pallas_call(
        unpack_kernel,
        in_specs=[VMEM],
        out_specs=(ANY,) * 4,
        out_shape=(jax.ShapeDtypeStruct((CHUNK, PLANE * HD), BF16),) * 4,
        scratch_shapes=[pltpu.VMEM((4, CHUNK, PLANE * HD), BF16), pltpu.SemaphoreType.DMA((4,))],
        compiler_params=room(6),
        name="unpack",
    )(near(packed))


def nt(a, b):
    return lax.dot_general(a, b, (((1,), (1,)), ((), ())), preferred_element_type=F32)


def nn(a, b):
    return lax.dot_general(a, b, (((1,), (0,)), ((), ())), preferred_element_type=F32)


def group_rows(x):
    return x.reshape(x.shape[0] // 8, 8, x.shape[1])


def marks(shape, dim, row):
    return (lax.broadcasted_iota(jnp.int32, shape, dim) == row).astype(F32)


SPANS = ((0, 2 * BLOCK), (0, 3 * BLOCK), (BLOCK, 2 * BLOCK))


def tokens(ref):
    return ref.reshape(ref.shape[0] * ref.shape[1], HD)


def keys(s, lo, n):
    return slice(s * FRAME + lo, s * FRAME + lo + n)


def block(r):
    return slice(r * BLOCK, (r + 1) * BLOCK)


def fetch(ref, index, a, dst):
    for h in range(CHUNKS):
        dst[h] = ref[index * CHUNKS + h, a]


def put(src, ref, index, a):
    for h in range(CHUNKS):
        ref[index * CHUNKS + h, a] = src[h]


def tile_bias(listed, frame, keyed):
    tiles = listed.shape[1]
    slot = lax.broadcasted_iota(jnp.int32, (HD, 1), 0)
    base = jnp.zeros_like(slot)
    for i, k in enumerate(keyed):
        base = jnp.where(slot // TILES_F == i, k, base)
    tile = base * TILES_F + slot % TILES_F
    tile = jnp.where(tile < 0, -TILES_F, tile)
    hit = jnp.zeros((HD, tiles), F32)
    for j in range(listed.shape[0]):
        hit = jnp.where(listed[j : j + 1, :] == tile, 1.0, hit)
    owner = lax.broadcasted_iota(jnp.int32, (tiles, FRAME), 1) // TILE + frame * TILES_F
    spread = (owner == lax.broadcasted_iota(jnp.int32, (tiles, FRAME), 0)).astype(F32).astype(BF16)
    return jnp.where(nn(hit.astype(BF16), spread) > 0.5, 0.0, MASKED).astype(BF16)


def set_hot(hot):
    lane = lax.broadcasted_iota(jnp.int32, (TILE, HD), 1)
    for t in range(3 * TILES_F):
        hot[t * TILE : (t + 1) * TILE, :] = (lane == t).astype(F32).astype(BF16)


class Scores:
    def __init__(self, slots, k, hot, vt, qt, s, p):
        self.slots, self.k, self.hot, self.vt, self.qt, self.s, self.p = slots, k, hot, vt, qt, s, p
        self.tops, self.sums = {}, {}
        vt[HD:, :] = marks((16, vt.shape[1]), 0, 0).astype(BF16)

    def score(self, r, i):
        lo, n = SPANS[r]
        kf = tokens(self.k)
        qt = self.qt[:, block(r)]
        for b in range(n // BLOCK):
            ks = keys(i, lo + b * BLOCK, BLOCK)
            hs = keys(self.slots[i], lo + b * BLOCK, BLOCK)
            st = nn(jnp.concatenate([kf[ks, :], self.hot[hs, :]], axis=1), qt)
            self.s[r, i * n + b * BLOCK : i * n + (b + 1) * BLOCK, :] = st
            got = jnp.max(group_rows(st), axis=0)
            self.tops[r] = jnp.maximum(self.tops[r], got) if r in self.tops else got
        if i == len(self.slots) - 1:
            self.tops[r] = jnp.max(self.tops[r], axis=0, keepdims=True) * (SCALE * LOG2E)

    def soften(self, r, i):
        lo, n = SPANS[r]
        for t in range(n // TILE):
            x = self.s[r, i * n + t * TILE : i * n + (t + 1) * TILE, :]
            e = jnp.exp2(x * (SCALE * LOG2E) - self.tops[r])
            self.p[i][lo + t * TILE : lo + (t + 1) * TILE, block(r)] = e.astype(BF16)
        got = nn(self.vt[:, keys(i, lo, n)], self.p[i][lo : lo + n, block(r)])
        self.sums[r] = self.sums[r] + got if r in self.sums else got


def settle(ot, r, ct, out_ref, *shares):
    cols = block(r)
    inv = 1.0 / ot[HD : HD + 1]
    out = (ot[:HD] * inv).astype(BF16)
    tokens(out_ref)[cols, :] = out.T
    for share, c2_ref in shares:
        factor = inv * SCALE if share is None else inv * SCALE * share
        c2 = (ct[:, cols].astype(F32) * factor).astype(BF16)
        c2_ref[:HD, cols] = c2
        dots = -jnp.sum(c2.astype(F32) * out.astype(F32), axis=0, keepdims=True)
        high = dots.astype(BF16).astype(F32)
        mid = (dots - high).astype(BF16).astype(F32)
        low = dots - high - mid
        shape = (HD, BLOCK)
        tail = marks(shape, 0, 0) * high + marks(shape, 0, 1) * mid + marks(shape, 0, 2) * low
        c2_ref[HD:, cols] = tail.astype(BF16)


class Grads:
    def __init__(self, v, kt, qt, c2, p, d):
        self.v, self.kt, self.qt, self.c2, self.p, self.d = v, kt, qt, c2, p, d
        self.sums = {}
        self.unit = (lax.broadcasted_iota(jnp.int32, (BLOCK, HD), 1) < 3).astype(F32).astype(BF16)

    def back(self, r, s):
        lo, n = SPANS[r]
        cols = block(r)
        vf = tokens(self.v)
        for b in range(n // BLOCK):
            at = slice(lo + b * BLOCK, lo + (b + 1) * BLOCK)
            rows = jnp.concatenate([vf[keys(s, lo + b * BLOCK, BLOCK), :], self.unit], axis=1)
            dp = nn(rows, self.c2[:, cols])
            self.d[s][at, cols] = self.p[s][at, cols] * dp.astype(BF16)
        got = nn(self.kt[:, keys(s, lo, n)], self.d[s][lo : lo + n, cols])
        self.sums[r] = self.sums[r] + got if r in self.sums else got

    def keyed(self, s, a):
        for b, (lo, n) in enumerate(SPANS):
            if a == 0:
                g = nt(self.qt[:HD, lo : lo + n], self.d[s][block(b), lo : lo + n])
            else:
                g = nt(self.c2[:HD, lo : lo + n], self.p[s][block(b), lo : lo + n]) * (1.0 / SCALE)
            yield block(b), g.astype(BF16).T


def early_kernel(
    mine_ref, swap_ref, near_ref,
    out_ref, p_ref, d_ref, qt_ref, c2_ref, ep_ref, eqt_ref, ect_ref, etop_ref, esum_ref,
    q_s, c_s, o_s, eq_s, ec_s, k_s, v_s, ek_s, ev_s, hot_s, kt_s, vt_s, evt_s, ct_s, s_s, es_s,
):
    core, first = lax.axis_index("co"), 4 * lax.axis_index("sx")
    partner = first + 1 - core
    local, outer = first + 2 - core, first + 3 * core
    frame = 1 - core
    fetch(mine_ref, frame, 0, q_s)
    for a, (dst, edst) in enumerate(((k_s, ek_s), (v_s, ev_s))):
        for h in range(CHUNKS):
            dst[h] = swap_ref[h, a]
            dst[CHUNKS + h] = mine_ref[frame * CHUNKS + h, 1 + a]
            dst[2 * CHUNKS + h] = swap_ref[CHUNKS + h, a]
            edst[h] = mine_ref[core * CHUNKS + h, 1 + a]
            edst[CHUNKS + h] = swap_ref[core * CHUNKS + h, a]
    fetch(mine_ref, frame, 3, c_s)
    fetch(mine_ref, core, 0, eq_s)
    fetch(mine_ref, core, 3, ec_s)
    set_hot(hot_s)
    listed = near_ref[...]
    qt_ref[:HD, :] = tokens(q_s)[...].T
    qt_ref[HD:, :] = tile_bias(listed, local, (partner, local, partner + 2))
    ps, ds = [p_ref.at[s] for s in range(3)], [d_ref.at[s] for s in range(3)]
    sc = Scores((0, 1, 2), k_s, hot_s, vt_s, qt_ref, s_s, ps)
    gr = Grads(v_s, kt_s, qt_ref, c2_ref, ps, ds)
    es = Scores((1, 2), ek_s, hot_s, evt_s, eqt_ref, es_s, [ep_ref.at[s] for s in range(2)])
    for s in range(3):
        sc.score(0, s)
    vt_s[:HD, :] = tokens(v_s)[...].T
    ct_s[...] = tokens(c_s)[...].T
    for s in range(3):
        sc.score(1, s)
        sc.soften(0, s)
    settle(sc.sums[0], 0, ct_s, o_s, (None, c2_ref))
    for s in range(3):
        sc.score(2, s)
        sc.soften(1, s)
    settle(sc.sums[1], 1, ct_s, o_s, (None, c2_ref))
    kt_s[...] = tokens(k_s)[...].T
    for s in range(3):
        gr.back(0, s)
        sc.soften(2, s)
    settle(sc.sums[2], 2, ct_s, o_s, (None, c2_ref))
    eqt_ref[:HD, :] = tokens(eq_s)[...].T
    eqt_ref[HD:, :] = tile_bias(listed, outer, (first - 1 + 5 * core, outer, partner + 2 * core))
    evt_s[:HD, :] = tokens(ev_s)[...].T
    ect_ref[...] = tokens(ec_s)[...].T
    for s in range(2):
        es.score(0, s)
    for s in range(2):
        es.score(1, s)
        es.soften(0, s)
        gr.back(1, s)
    gr.back(1, 2)
    for s in range(2):
        es.score(2, s)
        es.soften(1, s)
        gr.back(2, s)
    gr.back(2, 2)
    for s in range(2):
        es.soften(2, s)
    for r in range(3):
        tokens(q_s)[block(r), :] = gr.sums[r].astype(BF16).T
        etop_ref[:, block(r)] = jnp.broadcast_to(es.tops[r], (8, BLOCK))
        esum_ref[:, block(r)] = es.sums[r]
    put(o_s, out_ref, 0, 0)
    put(q_s, out_ref, 0, 1)


def outer_kernel(
    edge_ref, eqt_ref, ect_ref, etop_ref, esum_ref, out_ref, c2_ref, dqt_ref, gedge_ref,
    o_s, g_s, k_s, v_s, hot_s, kt_s, vt_s, c2_s, s_s, p_s, d_s,
):
    for a, dst in ((0, k_s), (1, v_s)):
        fetch(edge_ref, 0, a, dst)
    set_hot(hot_s)
    sc = Scores((0,), k_s, hot_s, vt_s, eqt_ref, s_s, [p_s])
    gr = Grads(v_s, kt_s, eqt_ref, c2_s, [p_s], [d_s])
    sc.score(0, 0)
    vt_s[:HD, :] = tokens(v_s)[...].T
    sc.score(1, 0)
    kt_s[...] = tokens(k_s)[...].T
    sc.score(2, 0)
    for r in range(3):
        sc.soften(r, 0)
    for r in range(3):
        old = etop_ref[0:1, block(r)]
        top = jnp.maximum(old, sc.tops[r])
        mine, edge = jnp.exp2(old - top), jnp.exp2(sc.tops[r] - top)
        total = esum_ref[:, block(r)] * mine + sc.sums[r] * edge
        settle(total, r, ect_ref, o_s, (edge, c2_s), (mine, c2_ref))
    for r in range(3):
        gr.back(r, 0)
    for r in range(3):
        dqt_ref[:, block(r)] = gr.sums[r]
    put(o_s, out_ref, 0, 0)
    for a in range(2):
        for rows, g in gr.keyed(0, a):
            tokens(g_s.at[a])[rows, :] = g
        put(g_s.at[a], gedge_ref, 0, a)


def late_kernel(
    mine_ref, swap_ref, ep_ref, eqt_ref, c2_ref, dqt_ref, lp_ref, ld_ref, lqt_ref, lc2_ref,
    dq_ref, lown_ref, gown_ref, gswap_ref, g_s, old_s, k_s, v_s, kt_s, d_s,
):
    core = lax.axis_index("co")
    for a, dst in ((0, k_s), (1, v_s)):
        for h in range(CHUNKS):
            dst[h] = mine_ref[core * CHUNKS + h, 1 + a]
            dst[CHUNKS + h] = swap_ref[core * CHUNKS + h, a]
    gr = Grads(v_s, kt_s, eqt_ref, c2_ref, [ep_ref.at[s] for s in range(2)], [d_s.at[s] for s in range(2)])
    done = Grads(None, None, lqt_ref, lc2_ref, [lp_ref.at[s] for s in range(3)], [ld_ref.at[s] for s in range(3)])
    kt_s[...] = tokens(k_s)[...].T
    for r in range(3):
        for s in range(2):
            gr.back(r, s)
    for r in range(3):
        tokens(g_s.at[0, 0])[block(r), :] = (gr.sums[r] + dqt_ref[:, block(r)]).astype(BF16).T
    for h in range(CHUNKS):
        dq_ref[h] = g_s[0, 0, h]
    for a in range(2):
        for i in range(2):
            for rows, g in done.keyed(2 * i, a):
                tokens(old_s.at[a, i])[rows, :] = g
        for rows, g in gr.keyed(1, a):
            tokens(g_s.at[a, 1])[rows, :] = g
        for h in range(CHUNKS):
            both = g_s[a, 1, h].astype(F32) + old_s[a, core, h].astype(F32)
            gswap_ref[core * CHUNKS + h, a] = both.astype(BF16)
            gswap_ref[(1 - core) * CHUNKS + h, a] = old_s[a, 1 - core, h]
    for a in range(2):
        for source, ref, s in ((gr, gown_ref, 0), (done, lown_ref, 1)):
            for rows, g in source.keyed(s, a):
                tokens(g_s.at[a, s])[rows, :] = g
            for h in range(CHUNKS):
                ref[h, a] = g_s[a, s, h]


PAIR = jax.ShapeDtypeStruct((PLANE, 2, CHUNK, HD), BF16)
HALF = jax.ShapeDtypeStruct((CHUNKS, 2, CHUNK, HD), BF16)
ONE = jax.ShapeDtypeStruct((CHUNKS, CHUNK, HD), BF16)


def frames(*shape):
    return pltpu.VMEM((*shape, CHUNK, HD), BF16)


def wide(rows):
    return pltpu.VMEM((rows, FRAME), BF16)


def held(*shape):
    return jax.ShapeDtypeStruct(shape, BF16)


def attend_early(mine, swap, neighbours):
    return pl.pallas_call(
        early_kernel,
        in_specs=[VMEM] * 3,
        out_specs=(VMEM,) * 10,
        out_shape=(
            HALF,
            held(3, FRAME, FRAME),
            held(3, FRAME, FRAME),
            held(2 * HD, FRAME),
            held(2 * HD, FRAME),
            held(2, FRAME, FRAME),
            held(2 * HD, FRAME),
            held(HD, FRAME),
            jax.ShapeDtypeStruct((8, FRAME), F32),
            jax.ShapeDtypeStruct((HD + 16, FRAME), F32),
        ),
        scratch_shapes=[frames(CHUNKS)] * 5
        + [frames(3 * CHUNKS)] * 2
        + [frames(2 * CHUNKS)] * 2
        + [
            pltpu.VMEM((KEYS, HD), BF16),
            pltpu.VMEM((HD, KEYS), BF16),
            pltpu.VMEM((HD + 16, KEYS), BF16),
            pltpu.VMEM((HD + 16, 2 * FRAME), BF16),
            wide(HD),
            pltpu.VMEM((3, 9 * BLOCK, BLOCK), F32),
            pltpu.VMEM((3, 6 * BLOCK, BLOCK), F32),
        ],
        compiler_params=room(34),
        name="attend_early",
    )(near(mine), near(swap), neighbours.T)


def attend_outer(edge, *kept):
    return pl.pallas_call(
        outer_kernel,
        in_specs=[VMEM] * 5,
        out_specs=(VMEM,) * 4,
        out_shape=(
            held(CHUNKS, 1, CHUNK, HD),
            held(2 * HD, FRAME),
            jax.ShapeDtypeStruct((HD, FRAME), F32),
            HALF,
        ),
        scratch_shapes=[
            frames(CHUNKS),
            frames(2, CHUNKS),
            frames(CHUNKS),
            frames(CHUNKS),
            pltpu.VMEM((KEYS, HD), BF16),
            wide(HD),
            wide(HD + 16),
            wide(2 * HD),
            pltpu.VMEM((3, 3 * BLOCK, BLOCK), F32),
            wide(FRAME),
            wide(FRAME),
        ],
        compiler_params=room(16),
        name="attend_outer",
    )(near(edge), *kept)


def attend_late(mine, swap, *kept):
    return pl.pallas_call(
        late_kernel,
        in_specs=[VMEM] * 10,
        out_specs=(VMEM,) * 4,
        out_shape=(ONE, HALF, HALF, PAIR),
        scratch_shapes=[
            frames(2, 2, CHUNKS),
            frames(2, 2, CHUNKS),
            frames(2 * CHUNKS),
            frames(2 * CHUNKS),
            pltpu.VMEM((HD, 2 * FRAME), BF16),
            pltpu.VMEM((2, FRAME, FRAME), BF16),
        ],
        compiler_params=room(14),
        name="attend_late",
    )(near(mine), near(swap), *kept)


def join_kernel(local_ref, outer_ref, dq_ref, lown_ref, eown_ref, swap_ref, edge_ref, out_ref):
    core = lax.axis_index("co")
    for h in range(CHUNKS):
        here, there = core * CHUNKS + h, (1 - core) * CHUNKS + h
        out_ref[there, 0] = local_ref[h, 0]
        out_ref[there, 1] = local_ref[h, 1]
        out_ref[here, 0] = outer_ref[h, 0]
        out_ref[here, 1] = dq_ref[h]
        for a in range(2):
            x = lown_ref[h, a].astype(F32) + swap_ref[there, a].astype(F32)
            out_ref[there, 2 + a] = x.astype(BF16)
            x = eown_ref[h, a].astype(F32) + swap_ref[here, a].astype(F32)
            out_ref[here, 2 + a] = (x + edge_ref[h, a].astype(F32)).astype(BF16)


def join(*parts):
    swap, edge = parts[-2:]
    return pl.pallas_call(
        join_kernel,
        in_specs=[VMEM] * 7,
        out_specs=VMEM,
        out_shape=jax.ShapeDtypeStruct((PLANE, 4, CHUNK, HD), BF16),
        compiler_params=room(10),
        name="join",
    )(*parts[:-2], near(swap), near(edge))


def shards(queries, keys, values, cotangent, neighbours):
    plane = ("yl", "head")
    ring = lax.axis_size("sx")
    across = []
    for i in range(ring - 1):
        across.append((2 * i + 1, 2 * i + 2))
        across.append((2 * i + 2, 2 * i + 1))
    swap_pairs = [(0, 1), (1, 0)]
    core = lax.axis_index("co")
    sent = enter(queries, keys, values, cotangent)
    mine = lax.all_to_all(sent, plane, split_axis=0, concat_axis=0, tiled=True)
    kv = mine[:, 1:3]
    swap = lax.ppermute(kv, "co", swap_pairs)
    kv_edge = lax.dynamic_slice_in_dim(kv, core * CHUNKS, CHUNKS, 0)
    edge = lax.ppermute(kv_edge, ("sx", "co"), across)
    local, lp, ld, lqt, lc2, ep, eqt, *kept = attend_early(mine, swap, neighbours)
    outer, c2, dqt, gedge = attend_outer(edge, eqt, *kept)
    gedge_in = lax.ppermute(gedge, ("sx", "co"), across)
    dq, lown, eown, gswap = attend_late(mine, swap, ep, eqt, c2, dqt, lp, ld, lqt, lc2)
    gswap_in = lax.ppermute(gswap, "co", swap_pairs)
    packed = join(local, outer, dq, lown, eown, gswap_in, gedge_in)
    return unpack(lax.all_to_all(packed, plane, split_axis=0, concat_axis=0, tiled=True))


def solution(mesh):
    view = Mesh(mesh.devices.reshape(mesh.devices.shape[0] // 4, 2, 2, -1), ("sx", "yl", "co", "head"))
    rows = P(("sx", "yl", "co", "head"), None)
    return jax.shard_map(
        shards,
        mesh=view,
        in_specs=(rows,) * 4 + (P(),),
        out_specs=(rows,) * 4,
        check_vma=False,
    )
```

```python
import math

import jax
import jax.numpy as jnp
from jax import lax
from jax.experimental import pallas as pl
from jax.experimental.pallas import tpu as pltpu
from jax.sharding import Mesh, PartitionSpec as P


TILE = 64
TILES_F = 12
HD = 128
FRAME = TILE * TILES_F
BLOCK = 4 * TILE
KEYS = 3 * FRAME
CHUNKS = 8
CHUNK = FRAME // CHUNKS
PLANE = 16
MASKED = -1e30
USED = 48
SCALE = 1.0 / math.sqrt(HD)
LOG2E = 1.4426950408889634
ANY = pl.BlockSpec(memory_space=pl.ANY)
VMEM = pl.BlockSpec(memory_space=pltpu.VMEM)
F32 = jnp.float32
BF16 = jnp.bfloat16


def near(x):
    return pltpu.with_memory_space_constraint(x, pltpu.VMEM)


def far(x):
    return pltpu.with_memory_space_constraint(x, pltpu.HBM)


def room(mib):
    return pltpu.CompilerParams(vmem_limit_bytes=mib * 2**20)


def enter_kernel(q_ref, k_ref, v_ref, c_ref, out_ref, in_s, in_sem):
    ins = []
    for a, ref in enumerate((q_ref, k_ref, v_ref, c_ref)):
        ins.append(pltpu.make_async_copy(ref, in_s.at[a], in_sem.at[a]))
        ins[a].start()
    for a in range(4):
        ins[a].wait()
        for g in range(PLANE):
            out_ref[g, a] = in_s[a, :, g * HD : (g + 1) * HD]


def enter(*parts):
    return pl.pallas_call(
        enter_kernel,
        in_specs=[ANY] * 4,
        out_specs=VMEM,
        out_shape=jax.ShapeDtypeStruct((PLANE, 4, CHUNK, HD), BF16),
        scratch_shapes=[pltpu.VMEM((4, CHUNK, PLANE * HD), BF16), pltpu.SemaphoreType.DMA((4,))],
        compiler_params=room(8),
        name="enter",
    )(*(far(x) for x in parts))


def unpack_kernel(in_ref, *refs):
    outs, (rows_s, sem) = refs[:-2], refs[-2:]
    copies = []
    for a, ref in enumerate(outs):
        for g in range(PLANE):
            rows_s[a, :, g * HD : (g + 1) * HD] = in_ref[g, a]
        copies.append(pltpu.make_async_copy(rows_s.at[a], ref, sem.at[a]))
        copies[a].start()
    for cp in copies:
        cp.wait()


def unpack(packed):
    return pl.pallas_call(
        unpack_kernel,
        in_specs=[VMEM],
        out_specs=(ANY,) * 4,
        out_shape=(jax.ShapeDtypeStruct((CHUNK, PLANE * HD), BF16),) * 4,
        scratch_shapes=[pltpu.VMEM((4, CHUNK, PLANE * HD), BF16), pltpu.SemaphoreType.DMA((4,))],
        compiler_params=room(6),
        name="unpack",
    )(near(packed))


def nt(a, b):
    return lax.dot_general(a, b, (((1,), (1,)), ((), ())), preferred_element_type=F32)


def nn(a, b):
    return lax.dot_general(a, b, (((1,), (0,)), ((), ())), preferred_element_type=F32)


def group_rows(x):
    return x.reshape(x.shape[0] // 8, 8, x.shape[1])


def marks(shape, dim, row):
    return (lax.broadcasted_iota(jnp.int32, shape, dim) == row).astype(F32)


SPANS = ((0, 2 * BLOCK), (0, 3 * BLOCK), (BLOCK, 2 * BLOCK))


def tokens(ref):
    return ref.reshape(ref.shape[0] * ref.shape[1], HD)


def keys(s, lo, n):
    return slice(s * FRAME + lo, s * FRAME + lo + n)


def block(r):
    return slice(r * BLOCK, (r + 1) * BLOCK)


def fetch(ref, index, a, dst):
    for h in range(CHUNKS):
        dst[h] = ref[index * CHUNKS + h, a]


def put(src, ref, index, a):
    for h in range(CHUNKS):
        ref[index * CHUNKS + h, a] = src[h]


def tile_bias(listed, frame, keyed):
    tiles = listed.shape[1]
    slot = lax.broadcasted_iota(jnp.int32, (USED, 1), 0)
    base = jnp.zeros_like(slot)
    for i, k in enumerate(keyed):
        base = jnp.where(slot // TILES_F == i, k, base)
    tile = base * TILES_F + slot % TILES_F
    tile = jnp.where(tile < 0, -TILES_F, tile)
    hit = jnp.zeros((USED, tiles), F32)
    for j in range(listed.shape[0]):
        hit = jnp.where(listed[j : j + 1, :] == tile, 1.0, hit)
    owner = lax.broadcasted_iota(jnp.int32, (tiles, FRAME), 1) // TILE + frame * TILES_F
    spread = (owner == lax.broadcasted_iota(jnp.int32, (tiles, FRAME), 0)).astype(F32).astype(BF16)
    return jnp.where(nn(hit.astype(BF16), spread) > 0.5, 0.0, MASKED).astype(BF16)


def set_hot(hot, slots):
    lane = lax.broadcasted_iota(jnp.int32, (TILE, HD), 1)
    for t in range(slots * TILES_F):
        hot[t * TILE : (t + 1) * TILE, :] = (lane == t).astype(F32).astype(BF16)


def over_keys(wide_ref, parts, r):
    lo, n = SPANS[r]
    left = [wide_ref[:, keys(i, lo, n)] for i in range(len(parts))]
    right = [part[lo : lo + n, block(r)] for part in parts]
    return nn(jnp.concatenate(left, axis=1), jnp.concatenate(right, axis=0))


class Scores:
    def __init__(self, slots, k, hot, vt, qt, s, p):
        self.slots, self.k, self.hot, self.vt, self.qt, self.s, self.p = slots, k, hot, vt, qt, s, p
        self.tops, self.sums = {}, {}
        vt[HD:, :] = marks((16, vt.shape[1]), 0, 0).astype(BF16)

    def score(self, r, i):
        lo, n = SPANS[r]
        kf = tokens(self.k)
        qt = self.qt[:, block(r)]
        for b in range(n // BLOCK):
            ks = keys(i, lo + b * BLOCK, BLOCK)
            hs = keys(self.slots[i], lo + b * BLOCK, BLOCK)
            st = nn(jnp.concatenate([kf[ks, :], self.hot[hs, :]], axis=1), qt)
            self.s[r, i * n + b * BLOCK : i * n + (b + 1) * BLOCK, :] = st
        if i == len(self.slots) - 1:
            top = jnp.full((8, BLOCK), 2 * MASKED, F32)
            for t in range(len(self.slots) * n // TILE):
                top = jnp.maximum(top, jnp.max(group_rows(self.s[r, t * TILE : (t + 1) * TILE, :]), axis=0))
            self.tops[r] = jnp.max(top, axis=0, keepdims=True) * (SCALE * LOG2E)

    def soften(self, r, i):
        lo, n = SPANS[r]
        for t in range(n // TILE):
            x = self.s[r, i * n + t * TILE : i * n + (t + 1) * TILE, :]
            e = jnp.exp2(x * (SCALE * LOG2E) - self.tops[r])
            self.p[i][lo + t * TILE : lo + (t + 1) * TILE, block(r)] = e.astype(BF16)
        if i == len(self.slots) - 1:
            self.sums[r] = over_keys(self.vt, self.p, r)


def weigh(cols, ct, factor, out, c2_ref):
    c2 = (ct[:, cols].astype(F32) * factor).astype(BF16)
    c2_ref[:HD, cols] = c2
    dots = -jnp.sum(c2.astype(F32) * out.astype(F32), axis=0, keepdims=True)
    high = dots.astype(BF16).astype(F32)
    mid = (dots - high).astype(BF16).astype(F32)
    low = dots - high - mid
    shape = (HD, BLOCK)
    tail = marks(shape, 0, 0) * high + marks(shape, 0, 1) * mid + marks(shape, 0, 2) * low
    c2_ref[HD:, cols] = tail.astype(BF16)


def settle(ot, r, ct, out_ref, c2_ref):
    inv = 1.0 / ot[HD : HD + 1]
    out = (ot[:HD] * inv).astype(BF16)
    tokens(out_ref)[block(r), :] = out.T
    weigh(block(r), ct, inv * SCALE, out, c2_ref)


class Grads:
    def __init__(self, v, kt, qt, c2, p, d):
        self.v, self.kt, self.qt, self.c2, self.p, self.d = v, kt, qt, c2, p, d
        self.unit = (lax.broadcasted_iota(jnp.int32, (BLOCK, HD), 1) < 3).astype(F32).astype(BF16)

    def back(self, r, s, held=None):
        lo, n = SPANS[r]
        cols = block(r)
        vf = tokens(self.v)
        for b in range(n // BLOCK):
            at = slice(lo + b * BLOCK, lo + (b + 1) * BLOCK)
            value = vf[keys(s if held is None else held, lo + b * BLOCK, BLOCK), :]
            dp = nn(jnp.concatenate([value, self.unit], axis=1), self.c2[:, cols])
            self.d[s][at, cols] = self.p[s][at, cols] * dp.astype(BF16)

    def query(self, r):
        return over_keys(self.kt, self.d, r)

    def keyed(self, s, a):
        for b, (lo, n) in enumerate(SPANS):
            if a == 0:
                g = nt(self.qt[:HD, lo : lo + n], self.d[s][block(b), lo : lo + n])
            else:
                g = nt(self.c2[:HD, lo : lo + n], self.p[s][block(b), lo : lo + n]) * (1.0 / SCALE)
            yield block(b), g.astype(BF16).T


def early_kernel(
    mine_ref, swap_ref, near_ref,
    out_ref, p_ref, d_ref, qt_ref, c2_ref, ep_ref, eqt_ref, ect_ref, etop_ref, esum_ref,
    q_s, c_s, o_s, eq_s, ec_s, k_s, v_s, ek_s, ev_s, hot_s, vt_s, evt_s, ct_s, s_s, es_s,
):
    core, first = lax.axis_index("co"), 4 * lax.axis_index("sx")
    partner = first + 1 - core
    local, outer = first + 2 - core, first + 3 * core
    frame = 1 - core
    fetch(mine_ref, frame, 0, q_s)
    for a, (dst, edst) in enumerate(((k_s, ek_s), (v_s, ev_s))):
        for h in range(CHUNKS):
            dst[h] = swap_ref[h, a]
            dst[CHUNKS + h] = mine_ref[frame * CHUNKS + h, 1 + a]
            dst[2 * CHUNKS + h] = swap_ref[CHUNKS + h, a]
            edst[h] = mine_ref[core * CHUNKS + h, 1 + a]
            edst[CHUNKS + h] = swap_ref[core * CHUNKS + h, a]
    fetch(mine_ref, frame, 3, c_s)
    fetch(mine_ref, core, 0, eq_s)
    fetch(mine_ref, core, 3, ec_s)
    set_hot(hot_s, 3)
    listed = near_ref[...]
    qt_ref[:HD, :] = tokens(q_s)[...].T
    qt_ref[HD + USED :, :] = jnp.zeros((HD - USED, FRAME), BF16)
    qt_ref[HD : HD + USED, :] = tile_bias(listed, local, (partner, local, partner + 2))
    ps = [p_ref.at[s] for s in range(3)]
    sc = Scores((0, 1, 2), k_s, hot_s, vt_s, qt_ref, s_s, ps)
    gr = Grads(v_s, None, qt_ref, c2_ref, ps, [d_ref.at[0], None, d_ref.at[1]])
    es = Scores((1, 2), ek_s, hot_s, evt_s, eqt_ref, es_s, [ep_ref.at[s] for s in range(2)])
    for s in range(3):
        sc.score(0, s)
    vt_s[:HD, :] = tokens(v_s)[...].T
    ct_s[...] = tokens(c_s)[...].T
    for s in range(3):
        sc.score(1, s)
        sc.soften(0, s)
    settle(sc.sums[0], 0, ct_s, o_s, c2_ref)
    for s in range(3):
        sc.score(2, s)
        sc.soften(1, s)
    settle(sc.sums[1], 1, ct_s, o_s, c2_ref)
    for s in range(3):
        sc.soften(2, s)
        if s != 1:
            gr.back(0, s)
    settle(sc.sums[2], 2, ct_s, o_s, c2_ref)
    eqt_ref[:HD, :] = tokens(eq_s)[...].T
    eqt_ref[HD + USED :, :] = jnp.zeros((HD - USED, FRAME), BF16)
    eqt_ref[HD : HD + USED, :] = tile_bias(listed, outer, (first - 1 + 5 * core, outer, partner + 2 * core))
    evt_s[:HD, :] = tokens(ev_s)[...].T
    ect_ref[...] = tokens(ec_s)[...].T
    for s in range(2):
        es.score(0, s)
    for s in range(2):
        es.score(1, s)
        es.soften(0, s)
        gr.back(1, 2 * s)
    for s in range(2):
        es.score(2, s)
        es.soften(1, s)
        gr.back(2, 2 * s)
    for s in range(2):
        es.soften(2, s)
    for r in range(3):
        etop_ref[:, block(r)] = jnp.broadcast_to(es.tops[r], (8, BLOCK))
        esum_ref[:, block(r)] = es.sums[r]
    put(o_s, out_ref, 0, 0)


def outer_kernel(
    edge_ref, eqt_ref, ect_ref, etop_ref, esum_ref, outt_ref, factor_ref, d_ref, gedge_ref,
    g_s, k_s, v_s, hot_s, vt_s, c2_s, s_s, p_s,
):
    for a, dst in ((0, k_s), (1, v_s)):
        fetch(edge_ref, 0, a, dst)
    set_hot(hot_s, 1)
    sc = Scores((0,), k_s, hot_s, vt_s, eqt_ref, s_s, [p_s])
    gr = Grads(v_s, None, eqt_ref, c2_s, [p_s], [d_ref])
    sc.score(0, 0)
    vt_s[:HD, :] = tokens(v_s)[...].T
    sc.score(1, 0)
    sc.score(2, 0)
    for r in range(3):
        sc.soften(r, 0)
    for r in range(3):
        cols = block(r)
        old = etop_ref[0:1, cols]
        top = jnp.maximum(old, sc.tops[r])
        mine, edge = jnp.exp2(old - top), jnp.exp2(sc.tops[r] - top)
        total = esum_ref[:, cols] * mine + sc.sums[r] * edge
        inv = 1.0 / total[HD : HD + 1]
        out = (total[:HD] * inv).astype(BF16)
        outt_ref[:, cols] = out
        factor_ref[:, cols] = jnp.broadcast_to(inv * SCALE * mine, (8, BLOCK))
        weigh(cols, ect_ref, inv * SCALE * edge, out, c2_s)
    for r in range(3):
        gr.back(r, 0)
    for a in (1, 0):
        for rows, g in gr.keyed(0, a):
            tokens(g_s.at[a])[rows, :] = g
        put(g_s.at[a], gedge_ref, 0, a)


def share_kernel(
    swap_ref, ep_ref, eqt_ref, ect_ref, outt_ref, factor_ref, lp_ref, ld_ref, lqt_ref, lc2_ref,
    d_ref, gswap_ref, c2_ref, out_ref, g_s, old_s, v_s,
):
    core = lax.axis_index("co")
    for r in range(3):
        weigh(block(r), ect_ref, factor_ref[0:1, block(r)], outt_ref[:, block(r)], c2_ref)
        tokens(g_s.at[0])[block(r), :] = outt_ref[:, block(r)].T
    put(g_s.at[0], out_ref, 0, 0)
    fetch(swap_ref, core, 1, v_s)
    gr = Grads(v_s, None, eqt_ref, c2_ref, [ep_ref.at[1]], [d_ref])
    done = Grads(None, None, lqt_ref, lc2_ref, [lp_ref.at[0], lp_ref.at[2]], [ld_ref.at[0], ld_ref.at[1]])
    for r in range(3):
        gr.back(r, 0)
    for a in (1, 0):
        for i in range(2):
            for rows, g in done.keyed(i, a):
                tokens(old_s.at[a, i])[rows, :] = g
        for rows, g in gr.keyed(0, a):
            tokens(g_s.at[a])[rows, :] = g
        for h in range(CHUNKS):
            both = g_s[a, h].astype(F32) + old_s[a, core, h].astype(F32)
            gswap_ref[core * CHUNKS + h, a] = both.astype(BF16)
            gswap_ref[(1 - core) * CHUNKS + h, a] = old_s[a, 1 - core, h]


def late_kernel(
    mine_ref, swap_ref, edge_ref, ep_ref, eqt_ref, c2_ref, d0_ref, ed_ref, lp_ref, ld_ref, lqt_ref, lc2_ref,
    edq_ref, ldq_ref, eown_ref, lown_ref, g_s, k_s, v_s, lk_s, lv_s, kt_s, lkt_s, d_s, ld_s,
):
    core = lax.axis_index("co")
    frame = 1 - core
    for h in range(CHUNKS):
        v_s[h] = mine_ref[core * CHUNKS + h, 2]
        k_s[h] = edge_ref[h, 0]
        k_s[CHUNKS + h] = mine_ref[core * CHUNKS + h, 1]
        k_s[2 * CHUNKS + h] = swap_ref[core * CHUNKS + h, 0]
        lv_s[h] = mine_ref[frame * CHUNKS + h, 2]
        lk_s[h] = swap_ref[h, 0]
        lk_s[CHUNKS + h] = mine_ref[frame * CHUNKS + h, 1]
        lk_s[2 * CHUNKS + h] = swap_ref[CHUNKS + h, 0]
    gr = Grads(v_s, kt_s, eqt_ref, c2_ref, [None, ep_ref.at[0], None], [d0_ref, d_s, ed_ref])
    done = Grads(lv_s, lkt_s, lqt_ref, lc2_ref, [None, lp_ref.at[1], None], [ld_ref.at[0], ld_s, ld_ref.at[1]])
    kt_s[...] = tokens(k_s)[...].T
    lkt_s[...] = tokens(lk_s)[...].T
    for r in range(3):
        gr.back(r, 1, 0)
        done.back(r, 1, 0)
    for r in range(3):
        tokens(g_s.at[0])[block(r), :] = gr.query(r).astype(BF16).T
        tokens(g_s.at[1])[block(r), :] = done.query(r).astype(BF16).T
    for h in range(CHUNKS):
        edq_ref[h] = g_s[0, h]
        ldq_ref[h] = g_s[1, h]
    for a in range(2):
        for i, (source, ref, s) in enumerate(((gr, eown_ref, 1), (done, lown_ref, 1))):
            for rows, g in source.keyed(s, a):
                tokens(g_s.at[2 + 2 * a + i])[rows, :] = g
            for h in range(CHUNKS):
                ref[h, a] = g_s[2 + 2 * a + i, h]


PAIR = jax.ShapeDtypeStruct((PLANE, 2, CHUNK, HD), BF16)
HALF = jax.ShapeDtypeStruct((CHUNKS, 2, CHUNK, HD), BF16)
ONE = jax.ShapeDtypeStruct((CHUNKS, CHUNK, HD), BF16)


def frames(*shape):
    return pltpu.VMEM((*shape, CHUNK, HD), BF16)


def wide(rows):
    return pltpu.VMEM((rows, FRAME), BF16)


def held(*shape):
    return jax.ShapeDtypeStruct(shape, BF16)


def attend_early(mine, swap, neighbours):
    return pl.pallas_call(
        early_kernel,
        in_specs=[VMEM] * 3,
        out_specs=(VMEM,) * 10,
        out_shape=(
            held(CHUNKS, 1, CHUNK, HD),
            held(3, FRAME, FRAME),
            held(2, FRAME, FRAME),
            held(2 * HD, FRAME),
            held(2 * HD, FRAME),
            held(2, FRAME, FRAME),
            held(2 * HD, FRAME),
            held(HD, FRAME),
            jax.ShapeDtypeStruct((8, FRAME), F32),
            jax.ShapeDtypeStruct((HD + 16, FRAME), F32),
        ),
        scratch_shapes=[frames(CHUNKS)] * 5
        + [frames(3 * CHUNKS)] * 2
        + [frames(2 * CHUNKS)] * 2
        + [
            pltpu.VMEM((KEYS, HD), BF16),
            pltpu.VMEM((HD + 16, KEYS), BF16),
            pltpu.VMEM((HD + 16, 2 * FRAME), BF16),
            wide(HD),
            pltpu.VMEM((3, 9 * BLOCK, BLOCK), F32),
            pltpu.VMEM((3, 6 * BLOCK, BLOCK), F32),
        ],
        compiler_params=room(34),
        name="attend_early",
    )(near(mine), near(swap), neighbours.T)


def attend_outer(edge, *kept):
    return pl.pallas_call(
        outer_kernel,
        in_specs=[VMEM] * 5,
        out_specs=(VMEM,) * 4,
        out_shape=(
            held(HD, FRAME),
            jax.ShapeDtypeStruct((8, FRAME), F32),
            held(FRAME, FRAME),
            HALF,
        ),
        scratch_shapes=[
            frames(2, CHUNKS),
            frames(CHUNKS),
            frames(CHUNKS),
            pltpu.VMEM((FRAME, HD), BF16),
            wide(HD + 16),
            wide(2 * HD),
            pltpu.VMEM((3, 3 * BLOCK, BLOCK), F32),
            wide(FRAME),
        ],
        compiler_params=room(16),
        name="attend_outer",
    )(near(edge), *kept)


def attend_share(swap, *kept):
    return pl.pallas_call(
        share_kernel,
        in_specs=[VMEM] * 10,
        out_specs=(VMEM,) * 4,
        out_shape=(held(FRAME, FRAME), PAIR, held(2 * HD, FRAME), held(CHUNKS, 1, CHUNK, HD)),
        scratch_shapes=[frames(2, CHUNKS), frames(2, 2, CHUNKS), frames(CHUNKS)],
        compiler_params=room(8),
        name="attend_share",
    )(near(swap), *kept)


def attend_late(mine, swap, edge, *kept):
    return pl.pallas_call(
        late_kernel,
        in_specs=[VMEM] * 12,
        out_specs=(VMEM,) * 4,
        out_shape=(ONE, ONE, HALF, HALF),
        scratch_shapes=[
            frames(6, CHUNKS),
            frames(3 * CHUNKS),
            frames(CHUNKS),
            frames(3 * CHUNKS),
            frames(CHUNKS),
            pltpu.VMEM((HD, KEYS), BF16),
            pltpu.VMEM((HD, KEYS), BF16),
            wide(FRAME),
            wide(FRAME),
        ],
        compiler_params=room(14),
        name="attend_late",
    )(near(mine), near(swap), near(edge), *kept)


def join_kernel(local_ref, outer_ref, ldq_ref, edq_ref, lown_ref, eown_ref, swap_ref, edge_ref, out_ref):
    core = lax.axis_index("co")
    for h in range(CHUNKS):
        here, there = core * CHUNKS + h, (1 - core) * CHUNKS + h
        out_ref[there, 0] = local_ref[h, 0]
        out_ref[there, 1] = ldq_ref[h]
        out_ref[here, 0] = outer_ref[h, 0]
        out_ref[here, 1] = edq_ref[h]
        for a in range(2):
            x = lown_ref[h, a].astype(F32) + swap_ref[there, a].astype(F32)
            out_ref[there, 2 + a] = x.astype(BF16)
            x = eown_ref[h, a].astype(F32) + swap_ref[here, a].astype(F32)
            out_ref[here, 2 + a] = (x + edge_ref[h, a].astype(F32)).astype(BF16)


def join(*parts):
    swap, edge = parts[-2:]
    return pl.pallas_call(
        join_kernel,
        in_specs=[VMEM] * 8,
        out_specs=VMEM,
        out_shape=jax.ShapeDtypeStruct((PLANE, 4, CHUNK, HD), BF16),
        compiler_params=room(10),
        name="join",
    )(*parts[:-2], near(swap), near(edge))


def shards(queries, keys, values, cotangent, neighbours):
    plane = ("yl", "head")
    ring = lax.axis_size("sx")
    across = []
    for i in range(ring - 1):
        across.append((2 * i + 1, 2 * i + 2))
        across.append((2 * i + 2, 2 * i + 1))
    swap_pairs = [(0, 1), (1, 0)]
    core = lax.axis_index("co")
    sent = enter(queries, keys, values, cotangent)
    mine = lax.all_to_all(sent, plane, split_axis=0, concat_axis=0, tiled=True)
    kv = mine[:, 1:3]
    swap = lax.ppermute(kv, "co", swap_pairs)
    kv_edge = lax.dynamic_slice_in_dim(kv, core * CHUNKS, CHUNKS, 0)
    edge = lax.ppermute(kv_edge, ("sx", "co"), across)
    local, lp, ld, lqt, lc2, ep, eqt, *kept = attend_early(mine, swap, neighbours)
    ect = kept[0]
    outt, factor, d0, gedge = attend_outer(edge, eqt, *kept)
    gedge_in = lax.ppermute(gedge, ("sx", "co"), across)
    ed, gswap, c2, outer = attend_share(swap, ep, eqt, ect, outt, factor, lp, ld, lqt, lc2)
    gswap_in = lax.ppermute(gswap, "co", swap_pairs)
    edq, ldq, eown, lown = attend_late(mine, swap, edge, ep, eqt, c2, d0, ed, lp, ld, lqt, lc2)
    packed = join(local, outer, ldq, edq, lown, eown, gswap_in, gedge_in)
    return unpack(lax.all_to_all(packed, plane, split_axis=0, concat_axis=0, tiled=True))


def solution(mesh):
    view = Mesh(mesh.devices.reshape(mesh.devices.shape[0] // 4, 2, 2, -1), ("sx", "yl", "co", "head"))
    rows = P(("sx", "yl", "co", "head"), None)
    return jax.shard_map(
        shards,
        mesh=view,
        in_specs=(rows,) * 4 + (P(),),
        out_specs=(rows,) * 4,
        check_vma=False,
    )
```

```python
import math

import jax
import jax.numpy as jnp
from jax import lax
from jax.experimental import pallas as pl
from jax.experimental.pallas import tpu as pltpu
from jax.sharding import Mesh, PartitionSpec as P


TILE = 64
TILES_F = 12
HD = 128
FRAME = TILE * TILES_F
BLOCK = 4 * TILE
KEYS = 3 * FRAME
CHUNKS = 8
CHUNK = FRAME // CHUNKS
PLANE = 16
MASKED = -1e30
USED = 48
SCALE = 1.0 / math.sqrt(HD)
LOG2E = 1.4426950408889634
ANY = pl.BlockSpec(memory_space=pl.ANY)
VMEM = pl.BlockSpec(memory_space=pltpu.VMEM)
F32 = jnp.float32
BF16 = jnp.bfloat16


def near(x):
    return pltpu.with_memory_space_constraint(x, pltpu.VMEM)


def far(x):
    return pltpu.with_memory_space_constraint(x, pltpu.HBM)


def room(mib):
    return pltpu.CompilerParams(vmem_limit_bytes=mib * 2**20)


def enter_kernel(q_ref, k_ref, v_ref, c_ref, out_ref, in_s, in_sem):
    ins = []
    for a, ref in enumerate((q_ref, k_ref, v_ref, c_ref)):
        ins.append(pltpu.make_async_copy(ref, in_s.at[a], in_sem.at[a]))
        ins[a].start()
    for a in range(4):
        ins[a].wait()
        for g in range(PLANE):
            out_ref[g, a] = in_s[a, :, g * HD : (g + 1) * HD]


def enter(*parts):
    return pl.pallas_call(
        enter_kernel,
        in_specs=[ANY] * 4,
        out_specs=VMEM,
        out_shape=jax.ShapeDtypeStruct((PLANE, 4, CHUNK, HD), BF16),
        scratch_shapes=[pltpu.VMEM((4, CHUNK, PLANE * HD), BF16), pltpu.SemaphoreType.DMA((4,))],
        compiler_params=room(8),
        name="enter",
    )(*(far(x) for x in parts))


def unpack_kernel(in_ref, *refs):
    outs, (rows_s, sem) = refs[:-2], refs[-2:]
    copies = []
    for a, ref in enumerate(outs):
        for g in range(PLANE):
            rows_s[a, :, g * HD : (g + 1) * HD] = in_ref[g, a]
        copies.append(pltpu.make_async_copy(rows_s.at[a], ref, sem.at[a]))
        copies[a].start()
    for cp in copies:
        cp.wait()


def unpack(packed):
    return pl.pallas_call(
        unpack_kernel,
        in_specs=[VMEM],
        out_specs=(ANY,) * 4,
        out_shape=(jax.ShapeDtypeStruct((CHUNK, PLANE * HD), BF16),) * 4,
        scratch_shapes=[pltpu.VMEM((4, CHUNK, PLANE * HD), BF16), pltpu.SemaphoreType.DMA((4,))],
        compiler_params=room(6),
        name="unpack",
    )(near(packed))


def nt(a, b):
    return lax.dot_general(a, b, (((1,), (1,)), ((), ())), preferred_element_type=F32)


def nn(a, b):
    return lax.dot_general(a, b, (((1,), (0,)), ((), ())), preferred_element_type=F32)


def group_rows(x):
    return x.reshape(x.shape[0] // 8, 8, x.shape[1])


def marks(shape, dim, row):
    return (lax.broadcasted_iota(jnp.int32, shape, dim) == row).astype(F32)


SPANS = ((0, 2 * BLOCK), (0, 3 * BLOCK), (BLOCK, 2 * BLOCK))


def tokens(ref):
    return ref.reshape(ref.shape[0] * ref.shape[1], HD)


def keys(s, lo, n):
    return slice(s * FRAME + lo, s * FRAME + lo + n)


def block(r):
    return slice(r * BLOCK, (r + 1) * BLOCK)


def fetch(ref, index, a, dst):
    for h in range(CHUNKS):
        dst[h] = ref[index * CHUNKS + h, a]


def put(src, ref, index, a):
    for h in range(CHUNKS):
        ref[index * CHUNKS + h, a] = src[h]


def tile_bias(listed, frame, keyed):
    tiles = listed.shape[1]
    slot = lax.broadcasted_iota(jnp.int32, (USED, 1), 0)
    base = jnp.zeros_like(slot)
    for i, k in enumerate(keyed):
        base = jnp.where(slot // TILES_F == i, k, base)
    tile = base * TILES_F + slot % TILES_F
    tile = jnp.where(tile < 0, -TILES_F, tile)
    hit = jnp.zeros((USED, tiles), F32)
    for j in range(listed.shape[0]):
        hit = jnp.where(listed[j : j + 1, :] == tile, 1.0, hit)
    owner = lax.broadcasted_iota(jnp.int32, (tiles, FRAME), 1) // TILE + frame * TILES_F
    spread = (owner == lax.broadcasted_iota(jnp.int32, (tiles, FRAME), 0)).astype(F32).astype(BF16)
    return jnp.where(nn(hit.astype(BF16), spread) > 0.5, 0.0, MASKED).astype(BF16)


def set_hot(hot, slots):
    lane = lax.broadcasted_iota(jnp.int32, (TILE, HD), 1)
    for t in range(slots * TILES_F):
        hot[t * TILE : (t + 1) * TILE, :] = (lane == t).astype(F32).astype(BF16)


def over_keys(wide_ref, parts, r):
    lo, n = SPANS[r]
    left = [wide_ref[:, keys(i, lo, n)] for i in range(len(parts))]
    right = [part[lo : lo + n, block(r)] for part in parts]
    return nn(jnp.concatenate(left, axis=1), jnp.concatenate(right, axis=0))


class Scores:
    def __init__(self, slots, k, hot, vt, qt, s, p):
        self.slots, self.k, self.hot, self.vt, self.qt, self.s, self.p = slots, k, hot, vt, qt, s, p
        self.tops, self.sums = {}, {}
        vt[HD:, :] = marks((16, vt.shape[1]), 0, 0).astype(BF16)

    def score(self, r, i):
        lo, n = SPANS[r]
        kf = tokens(self.k)
        qt = self.qt[:, block(r)]
        for b in range(n // BLOCK):
            ks = keys(i, lo + b * BLOCK, BLOCK)
            hs = keys(self.slots[i], lo + b * BLOCK, BLOCK)
            st = nn(jnp.concatenate([kf[ks, :], self.hot[hs, :]], axis=1), qt)
            self.s[r, i * n + b * BLOCK : i * n + (b + 1) * BLOCK, :] = st
        if i == len(self.slots) - 1:
            top = jnp.full((8, BLOCK), 2 * MASKED, F32)
            for t in range(len(self.slots) * n // TILE):
                top = jnp.maximum(top, jnp.max(group_rows(self.s[r, t * TILE : (t + 1) * TILE, :]), axis=0))
            self.tops[r] = jnp.max(top, axis=0, keepdims=True) * (SCALE * LOG2E)

    def soften(self, r, i):
        lo, n = SPANS[r]
        for t in range(n // TILE):
            x = self.s[r, i * n + t * TILE : i * n + (t + 1) * TILE, :]
            e = jnp.exp2(x * (SCALE * LOG2E) - self.tops[r])
            self.p[i][lo + t * TILE : lo + (t + 1) * TILE, block(r)] = e.astype(BF16)
        if i == len(self.slots) - 1:
            self.sums[r] = over_keys(self.vt, self.p, r)


def weigh(cols, ct, factor, out, c2_ref):
    c2 = (ct[:, cols].astype(F32) * factor).astype(BF16)
    c2_ref[:HD, cols] = c2
    dots = -jnp.sum(c2.astype(F32) * out.astype(F32), axis=0, keepdims=True)
    high = dots.astype(BF16).astype(F32)
    mid = (dots - high).astype(BF16).astype(F32)
    low = dots - high - mid
    shape = (HD, BLOCK)
    tail = marks(shape, 0, 0) * high + marks(shape, 0, 1) * mid + marks(shape, 0, 2) * low
    c2_ref[HD:, cols] = tail.astype(BF16)


def settle(ot, r, ct, out_ref, c2_ref):
    inv = 1.0 / ot[HD : HD + 1]
    out = (ot[:HD] * inv).astype(BF16)
    tokens(out_ref)[block(r), :] = out.T
    weigh(block(r), ct, inv * SCALE, out, c2_ref)


class Grads:
    def __init__(self, v, kt, qt, c2, p, d):
        self.v, self.kt, self.qt, self.c2, self.p, self.d = v, kt, qt, c2, p, d
        self.unit = (lax.broadcasted_iota(jnp.int32, (BLOCK, HD), 1) < 3).astype(F32).astype(BF16)

    def back(self, r, s, held=None):
        lo, n = SPANS[r]
        cols = block(r)
        vf = tokens(self.v)
        for b in range(n // BLOCK):
            at = slice(lo + b * BLOCK, lo + (b + 1) * BLOCK)
            value = vf[keys(s if held is None else held, lo + b * BLOCK, BLOCK), :]
            dp = nn(jnp.concatenate([value, self.unit], axis=1), self.c2[:, cols])
            self.d[s][at, cols] = self.p[s][at, cols] * dp.astype(BF16)

    def query(self, r):
        return over_keys(self.kt, self.d, r)

    def keyed(self, s, a):
        for b, (lo, n) in enumerate(SPANS):
            if a == 0:
                g = nt(self.qt[:HD, lo : lo + n], self.d[s][block(b), lo : lo + n])
            else:
                g = nt(self.c2[:HD, lo : lo + n], self.p[s][block(b), lo : lo + n]) * (1.0 / SCALE)
            yield block(b), g.astype(BF16).T


def early_kernel(
    mine_ref, swap_ref, near_ref,
    out_ref, p_ref, d_ref, qt_ref, c2_ref, ep_ref, eqt_ref, ect_ref, etop_ref, esum_ref,
    q_s, c_s, o_s, eq_s, ec_s, k_s, v_s, ek_s, ev_s, hot_s, vt_s, evt_s, ct_s, s_s, es_s,
):
    core, first = lax.axis_index("co"), 4 * lax.axis_index("sx")
    partner = first + 1 - core
    local, outer = first + 2 - core, first + 3 * core
    frame = 1 - core
    fetch(mine_ref, frame, 0, q_s)
    for a, (dst, edst) in enumerate(((k_s, ek_s), (v_s, ev_s))):
        for h in range(CHUNKS):
            dst[h] = swap_ref[h, a]
            dst[CHUNKS + h] = mine_ref[frame * CHUNKS + h, 1 + a]
            dst[2 * CHUNKS + h] = swap_ref[CHUNKS + h, a]
            edst[h] = mine_ref[core * CHUNKS + h, 1 + a]
            edst[CHUNKS + h] = swap_ref[core * CHUNKS + h, a]
    fetch(mine_ref, frame, 3, c_s)
    fetch(mine_ref, core, 0, eq_s)
    fetch(mine_ref, core, 3, ec_s)
    set_hot(hot_s, 3)
    listed = near_ref[...]
    qt_ref[:HD, :] = tokens(q_s)[...].T
    qt_ref[HD + USED :, :] = jnp.zeros((HD - USED, FRAME), BF16)
    qt_ref[HD : HD + USED, :] = tile_bias(listed, local, (partner, local, partner + 2))
    ps = [p_ref.at[s] for s in range(3)]
    sc = Scores((0, 1, 2), k_s, hot_s, vt_s, qt_ref, s_s, ps)
    gr = Grads(v_s, None, qt_ref, c2_ref, ps, [d_ref.at[0], None, d_ref.at[1]])
    es = Scores((1, 2), ek_s, hot_s, evt_s, eqt_ref, es_s, [ep_ref.at[s] for s in range(2)])
    for s in range(3):
        sc.score(0, s)
    vt_s[:HD, :] = tokens(v_s)[...].T
    ct_s[...] = tokens(c_s)[...].T
    for s in range(3):
        sc.score(1, s)
        sc.soften(0, s)
    settle(sc.sums[0], 0, ct_s, o_s, c2_ref)
    for s in range(3):
        sc.score(2, s)
        sc.soften(1, s)
    settle(sc.sums[1], 1, ct_s, o_s, c2_ref)
    for s in range(3):
        sc.soften(2, s)
        if s != 1:
            gr.back(0, s)
    settle(sc.sums[2], 2, ct_s, o_s, c2_ref)
    eqt_ref[:HD, :] = tokens(eq_s)[...].T
    eqt_ref[HD + USED :, :] = jnp.zeros((HD - USED, FRAME), BF16)
    eqt_ref[HD : HD + USED, :] = tile_bias(listed, outer, (first - 1 + 5 * core, outer, partner + 2 * core))
    evt_s[:HD, :] = tokens(ev_s)[...].T
    ect_ref[...] = tokens(ec_s)[...].T
    for s in range(2):
        es.score(0, s)
    for s in range(2):
        es.score(1, s)
        es.soften(0, s)
        gr.back(1, 2 * s)
    for s in range(2):
        es.score(2, s)
        es.soften(1, s)
        gr.back(2, 2 * s)
    for s in range(2):
        es.soften(2, s)
    for r in range(3):
        etop_ref[:, block(r)] = jnp.broadcast_to(es.tops[r], (8, BLOCK))
        esum_ref[:, block(r)] = es.sums[r]
    put(o_s, out_ref, 0, 0)


def outer_kernel(
    edge_ref, eqt_ref, ect_ref, etop_ref, esum_ref, outt_ref, factor_ref, d_ref, gedge_ref,
    g_s, k_s, v_s, hot_s, vt_s, c2_s, s_s, p_s,
):
    for a, dst in ((0, k_s), (1, v_s)):
        fetch(edge_ref, 0, a, dst)
    set_hot(hot_s, 1)
    sc = Scores((0,), k_s, hot_s, vt_s, eqt_ref, s_s, [p_s])
    gr = Grads(v_s, None, eqt_ref, c2_s, [p_s], [d_ref])
    sc.score(0, 0)
    vt_s[:HD, :] = tokens(v_s)[...].T
    sc.score(1, 0)
    sc.soften(0, 0)
    sc.score(2, 0)
    sc.soften(1, 0)
    sc.soften(2, 0)
    for r in range(3):
        cols = block(r)
        old = etop_ref[0:1, cols]
        top = jnp.maximum(old, sc.tops[r])
        mine, edge = jnp.exp2(old - top), jnp.exp2(sc.tops[r] - top)
        total = esum_ref[:, cols] * mine + sc.sums[r] * edge
        inv = 1.0 / total[HD : HD + 1]
        out = (total[:HD] * inv).astype(BF16)
        outt_ref[:, cols] = out
        factor_ref[:, cols] = jnp.broadcast_to(inv * SCALE * mine, (8, BLOCK))
        weigh(cols, ect_ref, inv * SCALE * edge, out, c2_s)
    value_terms = gr.keyed(0, 1)
    for r in range(3):
        gr.back(r, 0)
        rows, g = next(value_terms)
        tokens(g_s.at[1])[rows, :] = g
    put(g_s.at[1], gedge_ref, 0, 1)
    for rows, g in gr.keyed(0, 0):
        tokens(g_s.at[0])[rows, :] = g
    put(g_s.at[0], gedge_ref, 0, 0)


def share_kernel(
    swap_ref, ep_ref, eqt_ref, ect_ref, outt_ref, factor_ref, lp_ref, ld_ref, lqt_ref, lc2_ref,
    d_ref, gswap_ref, c2_ref, out_ref, g_s, old_s, v_s,
):
    core = lax.axis_index("co")
    for r in range(3):
        weigh(block(r), ect_ref, factor_ref[0:1, block(r)], outt_ref[:, block(r)], c2_ref)
        tokens(g_s.at[0])[block(r), :] = outt_ref[:, block(r)].T
    put(g_s.at[0], out_ref, 0, 0)
    fetch(swap_ref, core, 1, v_s)
    gr = Grads(v_s, None, eqt_ref, c2_ref, [ep_ref.at[1]], [d_ref])
    done = Grads(None, None, lqt_ref, lc2_ref, [lp_ref.at[0], lp_ref.at[2]], [ld_ref.at[0], ld_ref.at[1]])
    for r in range(3):
        gr.back(r, 0)
    for a in (1, 0):
        for i in range(2):
            for rows, g in done.keyed(i, a):
                tokens(old_s.at[a, i])[rows, :] = g
        for rows, g in gr.keyed(0, a):
            tokens(g_s.at[a])[rows, :] = g
        for h in range(CHUNKS):
            both = g_s[a, h].astype(F32) + old_s[a, core, h].astype(F32)
            gswap_ref[core * CHUNKS + h, a] = both.astype(BF16)
            gswap_ref[(1 - core) * CHUNKS + h, a] = old_s[a, 1 - core, h]


def late_kernel(
    mine_ref, swap_ref, edge_ref, ep_ref, eqt_ref, c2_ref, d0_ref, ed_ref, lp_ref, ld_ref, lqt_ref, lc2_ref,
    edq_ref, ldq_ref, eown_ref, lown_ref, g_s, k_s, v_s, lk_s, lv_s, kt_s, lkt_s, d_s, ld_s,
):
    core = lax.axis_index("co")
    frame = 1 - core
    for h in range(CHUNKS):
        v_s[h] = mine_ref[core * CHUNKS + h, 2]
        k_s[h] = edge_ref[h, 0]
        k_s[CHUNKS + h] = mine_ref[core * CHUNKS + h, 1]
        k_s[2 * CHUNKS + h] = swap_ref[core * CHUNKS + h, 0]
        lv_s[h] = mine_ref[frame * CHUNKS + h, 2]
        lk_s[h] = swap_ref[h, 0]
        lk_s[CHUNKS + h] = mine_ref[frame * CHUNKS + h, 1]
        lk_s[2 * CHUNKS + h] = swap_ref[CHUNKS + h, 0]
    gr = Grads(v_s, kt_s, eqt_ref, c2_ref, [None, ep_ref.at[0], None], [d0_ref, d_s, ed_ref])
    done = Grads(lv_s, lkt_s, lqt_ref, lc2_ref, [None, lp_ref.at[1], None], [ld_ref.at[0], ld_s, ld_ref.at[1]])
    kt_s[...] = tokens(k_s)[...].T
    lkt_s[...] = tokens(lk_s)[...].T
    for r in range(3):
        gr.back(r, 1, 0)
        done.back(r, 1, 0)
    for r in range(3):
        tokens(g_s.at[0])[block(r), :] = gr.query(r).astype(BF16).T
        tokens(g_s.at[1])[block(r), :] = done.query(r).astype(BF16).T
    for h in range(CHUNKS):
        edq_ref[h] = g_s[0, h]
        ldq_ref[h] = g_s[1, h]
    for a in range(2):
        for i, (source, ref, s) in enumerate(((gr, eown_ref, 1), (done, lown_ref, 1))):
            for rows, g in source.keyed(s, a):
                tokens(g_s.at[2 + 2 * a + i])[rows, :] = g
            for h in range(CHUNKS):
                ref[h, a] = g_s[2 + 2 * a + i, h]


PAIR = jax.ShapeDtypeStruct((PLANE, 2, CHUNK, HD), BF16)
HALF = jax.ShapeDtypeStruct((CHUNKS, 2, CHUNK, HD), BF16)
ONE = jax.ShapeDtypeStruct((CHUNKS, CHUNK, HD), BF16)


def frames(*shape):
    return pltpu.VMEM((*shape, CHUNK, HD), BF16)


def wide(rows):
    return pltpu.VMEM((rows, FRAME), BF16)


def held(*shape):
    return jax.ShapeDtypeStruct(shape, BF16)


def attend_early(mine, swap, neighbours):
    return pl.pallas_call(
        early_kernel,
        in_specs=[VMEM] * 3,
        out_specs=(VMEM,) * 10,
        out_shape=(
            held(CHUNKS, 1, CHUNK, HD),
            held(3, FRAME, FRAME),
            held(2, FRAME, FRAME),
            held(2 * HD, FRAME),
            held(2 * HD, FRAME),
            held(2, FRAME, FRAME),
            held(2 * HD, FRAME),
            held(HD, FRAME),
            jax.ShapeDtypeStruct((8, FRAME), F32),
            jax.ShapeDtypeStruct((HD + 16, FRAME), F32),
        ),
        scratch_shapes=[frames(CHUNKS)] * 5
        + [frames(3 * CHUNKS)] * 2
        + [frames(2 * CHUNKS)] * 2
        + [
            pltpu.VMEM((KEYS, HD), BF16),
            pltpu.VMEM((HD + 16, KEYS), BF16),
            pltpu.VMEM((HD + 16, 2 * FRAME), BF16),
            wide(HD),
            pltpu.VMEM((3, 9 * BLOCK, BLOCK), F32),
            pltpu.VMEM((3, 6 * BLOCK, BLOCK), F32),
        ],
        compiler_params=room(34),
        name="attend_early",
    )(near(mine), near(swap), neighbours.T)


def attend_outer(edge, *kept):
    return pl.pallas_call(
        outer_kernel,
        in_specs=[VMEM] * 5,
        out_specs=(VMEM,) * 4,
        out_shape=(
            held(HD, FRAME),
            jax.ShapeDtypeStruct((8, FRAME), F32),
            held(FRAME, FRAME),
            HALF,
        ),
        scratch_shapes=[
            frames(2, CHUNKS),
            frames(CHUNKS),
            frames(CHUNKS),
            pltpu.VMEM((FRAME, HD), BF16),
            wide(HD + 16),
            wide(2 * HD),
            pltpu.VMEM((3, 3 * BLOCK, BLOCK), F32),
            wide(FRAME),
        ],
        compiler_params=room(16),
        name="attend_outer",
    )(near(edge), *kept)


def attend_share(swap, *kept):
    return pl.pallas_call(
        share_kernel,
        in_specs=[VMEM] * 10,
        out_specs=(VMEM,) * 4,
        out_shape=(held(FRAME, FRAME), PAIR, held(2 * HD, FRAME), held(CHUNKS, 1, CHUNK, HD)),
        scratch_shapes=[frames(2, CHUNKS), frames(2, 2, CHUNKS), frames(CHUNKS)],
        compiler_params=room(8),
        name="attend_share",
    )(near(swap), *kept)


def attend_late(mine, swap, edge, *kept):
    return pl.pallas_call(
        late_kernel,
        in_specs=[VMEM] * 12,
        out_specs=(VMEM,) * 4,
        out_shape=(ONE, ONE, HALF, HALF),
        scratch_shapes=[
            frames(6, CHUNKS),
            frames(3 * CHUNKS),
            frames(CHUNKS),
            frames(3 * CHUNKS),
            frames(CHUNKS),
            pltpu.VMEM((HD, KEYS), BF16),
            pltpu.VMEM((HD, KEYS), BF16),
            wide(FRAME),
            wide(FRAME),
        ],
        compiler_params=room(14),
        name="attend_late",
    )(near(mine), near(swap), near(edge), *kept)


def join_kernel(local_ref, outer_ref, ldq_ref, edq_ref, lown_ref, eown_ref, swap_ref, edge_ref, out_ref):
    core = lax.axis_index("co")
    for h in range(CHUNKS):
        here, there = core * CHUNKS + h, (1 - core) * CHUNKS + h
        out_ref[there, 0] = local_ref[h, 0]
        out_ref[there, 1] = ldq_ref[h]
        out_ref[here, 0] = outer_ref[h, 0]
        out_ref[here, 1] = edq_ref[h]
        for a in range(2):
            x = lown_ref[h, a].astype(F32) + swap_ref[there, a].astype(F32)
            out_ref[there, 2 + a] = x.astype(BF16)
            x = eown_ref[h, a].astype(F32) + swap_ref[here, a].astype(F32)
            out_ref[here, 2 + a] = (x + edge_ref[h, a].astype(F32)).astype(BF16)


def join(*parts):
    swap, edge = parts[-2:]
    return pl.pallas_call(
        join_kernel,
        in_specs=[VMEM] * 8,
        out_specs=VMEM,
        out_shape=jax.ShapeDtypeStruct((PLANE, 4, CHUNK, HD), BF16),
        compiler_params=room(10),
        name="join",
    )(*parts[:-2], near(swap), near(edge))


def shards(queries, keys, values, cotangent, neighbours):
    plane = ("yl", "head")
    ring = lax.axis_size("sx")
    across = []
    for i in range(ring - 1):
        across.append((2 * i + 1, 2 * i + 2))
        across.append((2 * i + 2, 2 * i + 1))
    swap_pairs = [(0, 1), (1, 0)]
    core = lax.axis_index("co")
    sent = enter(queries, keys, values, cotangent)
    mine = lax.all_to_all(sent, plane, split_axis=0, concat_axis=0, tiled=True)
    kv = mine[:, 1:3]
    swap = lax.ppermute(kv, "co", swap_pairs)
    kv_edge = lax.dynamic_slice_in_dim(kv, core * CHUNKS, CHUNKS, 0)
    edge = lax.ppermute(kv_edge, ("sx", "co"), across)
    local, lp, ld, lqt, lc2, ep, eqt, *kept = attend_early(mine, swap, neighbours)
    ect = kept[0]
    outt, factor, d0, gedge = attend_outer(edge, eqt, *kept)
    gedge_in = lax.ppermute(gedge, ("sx", "co"), across)
    ed, gswap, c2, outer = attend_share(swap, ep, eqt, ect, outt, factor, lp, ld, lqt, lc2)
    gswap_in = lax.ppermute(gswap, "co", swap_pairs)
    edq, ldq, eown, lown = attend_late(mine, swap, edge, ep, eqt, c2, d0, ed, lp, ld, lqt, lc2)
    packed = join(local, outer, ldq, edq, lown, eown, gswap_in, gedge_in)
    return unpack(lax.all_to_all(packed, plane, split_axis=0, concat_axis=0, tiled=True))


def solution(mesh):
    view = Mesh(mesh.devices.reshape(mesh.devices.shape[0] // 4, 2, 2, -1), ("sx", "yl", "co", "head"))
    rows = P(("sx", "yl", "co", "head"), None)
    return jax.shard_map(
        shards,
        mesh=view,
        in_specs=(rows,) * 4 + (P(),),
        out_specs=(rows,) * 4,
        check_vma=False,
    )
```
